32 devices in a mesh: dp: 8 (over y, x, core), section: 4 (over z).
Axes of the slice: x: 2, y: 2, z: 4, core: 2. Of those that a mesh axis runs over, the one named last changes fastest.
Arguments:
- inputs: bfloat16 [1280, 8192], P('dp'), may hold values from -6 to 6
- cotangent: bfloat16 [1280, 8192], P('dp'), may hold values from -0.625 to 0.625
- weight_in: bfloat16 [4, 8192, 512], P('section'), may hold values from -0.0625 to 0.0625
- weight_out: bfloat16 [4, 8192, 512], P('section'), may hold values from -0.25 to 0.25
- norm_gains: float32 [4, 8192], P('section'), may hold values from 0.1 to 1.9
Outputs:
- in_grad: float32 [4, 8192, 512], P('section', 'dp')
- out_grad: float32 [4, 8192, 512], P('section', 'dp')
- gain_grad: float32 [4, 8192], P('section', 'dp')
The draws below stay inside these ranges and needn't reach their ends.
All inputs are finite; a program needn't handle non-finite values.
Results may differ from the reference program's by a relative error of at most 0.025.
Values may be sent and summed in bfloat16 or wider, within the bound.
A program may use at most 192 MiB of HBM per device.

```python
import jax
import jax.numpy as jnp
from jax import lax

D = 8192
H = 512
SECTIONS = 4
TOK_DEV = 160
TOKENS = 1280
N_DP = 8


def raised(values, stream_key, source, target, shards_of, factor):
    owner, partner = [(jnp.arange(values.shape[position]) // (values.shape[position] // shards_of)).reshape([-1 if axis == position else 1 for axis in range(values.ndim)]) for position in (source, target)]
    chosen = jax.random.permutation(stream_key, shards_of)[partner]
    strong = (owner == chosen) | (owner == (partner + shards_of // 2) % shards_of)
    return jnp.where(strong, factor * values, values)


def shard_levels(stream_key, extent, cuts, low, top_value):
    loudness, own = 1.0, jax.random.fold_in(stream_key, 6)
    for dim, parts in cuts:
        heights = jnp.exp(jax.random.uniform(jax.random.fold_in(own, dim), (parts,), jnp.float32, low / len(cuts), top_value / len(cuts)))
        loudness = loudness * jnp.repeat(heights, extent[dim] // parts).reshape([-1 if axis == dim else 1 for axis in range(len(extent))])
    return loudness


def scatter_about(stream_key, dims, deviation, bound, shards=(), held_as=jnp.bfloat16):
    result = deviation * jax.random.normal(stream_key, dims, jnp.float32)
    if shards:
        result = result * shard_levels(stream_key, dims, shards, -0.22, 0.18)
    return jnp.clip(result, -bound, bound).astype(held_as)


def noise_with(key, shape, deviation, limit, shards, heavy, held_as=jnp.bfloat16):
    result = deviation * jax.random.normal(key, shape, jnp.float32)
    if shards:
        result = result * shard_levels(key, shape, shards, -0.22, 0.18)
    return jnp.clip(raised(result, jax.random.fold_in(key, 3), *heavy), -limit, limit).astype(held_as)


def setup_inputs(seed: int = 0) -> dict:
    key_of = jax.random.split(jax.random.key(seed), 6)
    inputs = scatter_about(key_of[0], (TOKENS, D), 1.0, 6.0, ((0, 8),))
    cotangent = noise_with(key_of[1], (TOKENS, D), (TOKENS ** -0.5), 0.625, ((0, 8),), (0, 1, 8, 2.0))
    weight_in = scatter_about(key_of[2], (SECTIONS, D, H), D ** -0.5, 0.0625, ((0, 4),))
    weight_out = scatter_about(key_of[3], (SECTIONS, D, H), H ** -0.5, 0.25, ((0, 4),))
    norm_gains = jnp.clip(1.0 + 0.18 * jax.random.normal(key_of[4], (SECTIONS, D), jnp.float32), 0.1, 1.9)
    return {"inputs": inputs, "cotangent": cotangent, "weight_in": weight_in, "weight_out": weight_out, "norm_gains": norm_gains}


EPSILON = 1e-05

def normalize(block_rows, gain_row):
    values = block_rows.astype(jnp.float32)
    row_scale = lax.rsqrt(lax.optimization_barrier(jnp.mean(values * values, axis=1, keepdims=True)) + EPSILON)
    normed = (values * row_scale * gain_row).astype(jnp.bfloat16)
    return (values, row_scale, normed)

def layer_forward(block_rows, w_in, w_out, gain_row):
    values, row_scale, normed = normalize(block_rows, gain_row)
    pre_act = jnp.dot(normed, w_in, preferred_element_type=jnp.float32)
    activated = jax.nn.silu(pre_act).astype(jnp.bfloat16)
    branch = lax.dot_general(activated, w_out, (((1,), (1,)), ((), ())), preferred_element_type=jnp.float32)
    return (values + branch).astype(jnp.bfloat16)

def backward_parts(block_rows, upstream, w_in, w_out, gain_row):
    values, row_scale, normed = normalize(block_rows, gain_row)
    pre_act = jnp.dot(normed, w_in, preferred_element_type=jnp.float32)
    activated = jax.nn.silu(pre_act).astype(jnp.bfloat16)
    grad_act = jnp.dot(upstream, w_out, preferred_element_type=jnp.float32)
    sigmoid_pre = jax.nn.sigmoid(pre_act)
    grad_pre = (grad_act * sigmoid_pre * (1.0 + pre_act * (1.0 - sigmoid_pre))).astype(jnp.bfloat16)
    grad_norm = lax.dot_general(grad_pre, w_in, (((1,), (1,)), ((), ())), preferred_element_type=jnp.float32)
    scaled = grad_norm * gain_row
    centered = lax.optimization_barrier(jnp.mean(scaled * values, axis=1, keepdims=True))
    grad_in = (upstream.astype(jnp.float32) + row_scale * scaled - values * row_scale ** 3 * centered).astype(jnp.bfloat16)
    gain_rows = grad_norm * values * row_scale
    return (grad_in, normed, grad_pre, activated, gain_rows)

def column_product(left, right):
    return lax.dot_general(left, right, (((0,), (0,)), ((), ())), preferred_element_type=jnp.float32)

def reference(inputs, cotangent, weight_in, weight_out, norm_gains):
    hidden = [inputs]
    for section_id in range(SECTIONS - 1):
        hidden.append(layer_forward(hidden[-1], weight_in[section_id], weight_out[section_id], norm_gains[section_id]))
    upstream = cotangent
    in_list = [None] * SECTIONS
    out_list = [None] * SECTIONS
    gain_list = [None] * SECTIONS
    for section_id in reversed(range(SECTIONS)):
        grad_in, normed, grad_pre, activated, gain_rows = backward_parts(hidden[section_id], upstream, weight_in[section_id], weight_out[section_id], norm_gains[section_id])
        in_total = jnp.zeros((D, H), jnp.float32)
        out_total = jnp.zeros((D, H), jnp.float32)
        gain_total = jnp.zeros((D,), jnp.float32)
        for replica in range(N_DP):
            low = replica * TOK_DEV
            high = low + TOK_DEV
            in_term = column_product(normed[low:high], grad_pre[low:high])
            in_total = in_total + lax.optimization_barrier(in_term.astype(jnp.bfloat16)).astype(jnp.float32)
            out_term = column_product(upstream[low:high], activated[low:high])
            out_total = out_total + lax.optimization_barrier(out_term.astype(jnp.bfloat16)).astype(jnp.float32)
            gain_term = lax.optimization_barrier(jnp.sum(gain_rows[low:high], axis=0))
            gain_total = gain_total + lax.optimization_barrier(gain_term.astype(jnp.bfloat16)).astype(jnp.float32)
        in_list[section_id] = in_total
        out_list[section_id] = out_total
        gain_list[section_id] = gain_total
        upstream = grad_in
    return (jnp.stack(in_list), jnp.stack(out_list), jnp.stack(gain_list))
```

```python
import functools

import jax
import jax.numpy as jnp
from jax import lax
from jax.experimental import pallas as pl
from jax.experimental.pallas import tpu as pltpu
from jax.sharding import PartitionSpec as P

ROWS = 16
WCHUNK = 1024
DELAY = 1
EPSILON = 1e-05
MESH = pl.DeviceIdType.MESH


def nt_dot(left, right):
    return lax.dot_general(
        left, right, (((1,), (1,)), ((), ())), preferred_element_type=jnp.float32
    )


def relay_kernel(
    sections,
    replicas,
    micros,
    x_ref,
    c_ref,
    win_hbm,
    wout_hbm,
    gain_ref,
    all_h,
    all_g,
    all_act,
    all_du,
    win,
    wout,
    win_t,
    wout_t,
    stash,
    up,
    out_f,
    out_b,
    act_buf,
    du_buf,
    pre,
    scale,
    w_sem,
    f_recv,
    b_recv,
    f_send,
    b_send,
    x_recv,
    x_send,
):
    width = stash.shape[2]
    hidden = win.shape[1]
    quarter = width // 4
    pieces = ((0, quarter), (quarter, 2 * quarter), (3 * quarter, quarter))
    groups = ((0, 2), (2, 3))
    wchunks = width // WCHUNK
    pos = lax.axis_index("section")
    block = width // replicas
    me = lax.axis_index("dp")
    is_first = pos == 0
    is_last = pos == sections - 1
    not_first = pos > 0
    not_last = pos < sections - 1

    def wcopy(kind, i):
        rows = pl.ds(pl.multiple_of(i * WCHUNK, WCHUNK), WCHUNK)
        src, dst = ((win_hbm, win), (wout_hbm, wout))[kind]
        return pltpu.make_async_copy(src.at[rows, :], dst.at[rows, :], w_sem.at[kind, i])

    def load_weights(kind):
        @pl.loop(0, wchunks)
        def _(i):
            wcopy(kind, i).start()

    @pl.when(is_first)
    def _():
        for m in range(micros):
            for k, (start, size) in enumerate(pieces):
                pltpu.make_async_copy(
                    x_ref.at[m, :, pl.ds(start, size)],
                    stash.at[m, :, pl.ds(start, size)],
                    f_recv.at[m, k],
                ).start()
            if m == 0:
                load_weights(0)
                load_weights(1)

    @pl.when(not_first)
    def _():
        load_weights(1)
        load_weights(0)

    @pl.when(is_last)
    def _():
        for m in range(micros):
            for k, (start, size) in enumerate(pieces):
                pltpu.make_async_copy(
                    c_ref.at[m, :, pl.ds(start, size)],
                    up.at[m, :, pl.ds(start, size)],
                    b_recv.at[m, k],
                ).start()

    barrier = pltpu.get_barrier_semaphore()

    @pl.when(not_first)
    def _():
        pl.semaphore_signal(
            barrier, inc=1, device_id={"section": pos - 1}, device_id_type=MESH
        )

    @pl.when(not_last)
    def _():
        pl.semaphore_signal(
            barrier, inc=1, device_id={"section": pos + 1}, device_id_type=MESH
        )

    @pl.loop(1, replicas)
    def _(step):
        pl.semaphore_signal(
            barrier,
            inc=1,
            device_id={"dp": lax.rem(me + step, replicas)},
            device_id_type=MESH,
        )

    pl.semaphore_wait(
        barrier,
        replicas - 1 + not_first.astype(jnp.int32) + not_last.astype(jnp.int32),
    )

    @pl.when(not_first)
    def _():
        @pl.loop(0, wchunks)
        def _(i):
            wcopy(1, i).wait()

            @pl.when(not_last)
            def _():
                rows = pl.ds(pl.multiple_of(i * WCHUNK, WCHUNK), WCHUNK)
                wout_t[:, rows] = wout[rows, :].T

        @pl.loop(0, wchunks)
        def _(i):
            rows = pl.ds(pl.multiple_of(i * WCHUNK, WCHUNK), WCHUNK)
            wcopy(0, i).wait()
            win_t[:, rows] = win[rows, :].T

    def send_forward(m, k):
        start, size = pieces[k]
        return pltpu.make_async_remote_copy(
            src_ref=out_f.at[m, :, pl.ds(start, size)],
            dst_ref=stash.at[m, :, pl.ds(start, size)],
            send_sem=f_send.at[m, k],
            recv_sem=f_recv.at[m, k],
            device_id={"section": pos + 1},
            device_id_type=MESH,
        )

    def send_backward(m, k):
        start, size = pieces[k]
        return pltpu.make_async_remote_copy(
            src_ref=out_b.at[m, :, pl.ds(start, size)],
            dst_ref=up.at[m, :, pl.ds(start, size)],
            send_sem=b_send.at[m, k],
            recv_sem=b_recv.at[m, k],
            device_id={"section": pos - 1},
            device_id_type=MESH,
        )

    def arrived(buffer, sems, m, k):
        start, size = pieces[k]
        piece = buffer.at[m, :, pl.ds(start, size)]
        pltpu.make_async_copy(piece, piece, sems.at[m, k]).wait()

    def span(first, past):
        start = pieces[first][0]
        return start, pieces[past - 1][0] + pieces[past - 1][1] - start

    def share(kind, src_of, dst):
        pltpu.make_async_copy(src_of(me), dst, x_recv.at[kind]).start()

        @pl.loop(1, replicas)
        def _(step):
            peer = lax.rem(me + step, replicas)
            pltpu.make_async_remote_copy(
                src_ref=src_of(peer),
                dst_ref=dst,
                send_sem=x_send.at[kind],
                recv_sem=x_recv.at[kind],
                device_id={"dp": peer},
                device_id_type=MESH,
            ).start()

    def part(owner):
        return pl.ds(pl.multiple_of(owner * block, block), block)

    def forward(m):
        total = jnp.zeros((ROWS, 1), jnp.float32)
        u = jnp.zeros((ROWS, hidden), jnp.float32)
        for first, past in groups:
            start, size = span(first, past)
            for k in range(first, past):
                arrived(stash, f_recv, m, k)

            @pl.when((m == 0) & is_first)
            def _():
                @pl.loop(start // WCHUNK, (start + size) // WCHUNK)
                def _(i):
                    wcopy(0, i).wait()

            h = stash[m, :, start : start + size].astype(jnp.float32)
            scaled = (h * gain_ref[:, start : start + size]).astype(jnp.bfloat16)
            total = total + jnp.sum(h * h, axis=1, keepdims=True)
            u = u + jnp.dot(
                scaled, win[start : start + size, :], preferred_element_type=jnp.float32
            )
        inv = lax.rsqrt(total / width + EPSILON)
        u = u * inv
        act = (u * jax.nn.sigmoid(u)).astype(jnp.bfloat16)
        pre[m] = u
        scale[m] = jnp.broadcast_to(inv, scale.shape[1:])
        act_buf[m] = act

        @pl.when((m == 0) & is_first)
        def _():
            @pl.loop(0, wchunks)
            def _(i):
                wcopy(1, i).wait()

        def emit(product):
            for k, (start, size) in enumerate(pieces):
                cols = slice(start, start + size)
                h = stash[m, :, cols].astype(jnp.float32)
                out_f[m, :, cols] = (h + product(cols)).astype(jnp.bfloat16)
                send_forward(m, k).start()

        @pl.when(is_first)
        def _():
            emit(lambda cols: nt_dot(act, wout[cols, :]))

        @pl.when(not_first & not_last)
        def _():
            emit(
                lambda cols: jnp.dot(
                    act, wout_t[:, cols], preferred_element_type=jnp.float32
                )
            )

        share(0, lambda owner: stash.at[m, :, part(owner)], all_h.at[me, m])
        share(1, lambda owner: act_buf.at[m], all_act.at[me, m])

    def backward(m):
        da = jnp.zeros((ROWS, hidden), jnp.float32)
        for first, past in groups:
            start, size = span(first, past)
            for k in range(first, past):
                arrived(up, b_recv, m, k)
            da = da + jnp.dot(
                up[m, :, start : start + size],
                wout[start : start + size, :],
                preferred_element_type=jnp.float32,
            )
        u = pre[m]
        inv = scale[m][:, :1]
        sig = jax.nn.sigmoid(u)
        wide_du = da * sig * (1.0 + u * (1.0 - sig))
        du = wide_du.astype(jnp.bfloat16)
        du_buf[m] = (wide_du * inv).astype(jnp.bfloat16)
        centered = jnp.sum(du.astype(jnp.float32) * u, axis=1, keepdims=True) / (
            inv * width
        )
        pull = inv * inv * inv * centered

        @pl.when(not_first)
        def _():
            for k, (start, size) in enumerate(pieces):
                cols = slice(start, start + size)
                h = stash[m, :, cols].astype(jnp.float32)
                g = up[m, :, cols].astype(jnp.float32)
                dn = jnp.dot(du, win_t[:, cols], preferred_element_type=jnp.float32)
                out_b[m, :, cols] = (
                    g + inv * (dn * gain_ref[:, cols]) - h * pull
                ).astype(jnp.bfloat16)
                send_backward(m, k).start()

        share(2, lambda owner: up.at[m, :, part(owner)], all_g.at[me, m])
        share(3, lambda owner: du_buf.at[m], all_du.at[me, m])

    @pl.loop(0, micros + 2 * DELAY * (sections - 1))
    def _(tick):
        mf = tick - DELAY * pos
        mb = tick - DELAY * (2 * (sections - 1) - pos)

        @pl.when((mf >= 0) & (mf < micros))
        def _():
            forward(mf)

        @pl.when((mb >= 0) & (mb < micros))
        def _():
            backward(mb)

    @pl.loop(0, micros)
    def _(m):
        for k in range(len(pieces)):

            @pl.when(not_last)
            def _():
                send_forward(m, k).wait_send()

            @pl.when(not_first)
            def _():
                send_backward(m, k).wait_send()

    for kind, ref in enumerate((all_h, all_act, all_g, all_du)):
        sent = ref.at[pl.ds(0, replicas - 1)]
        pltpu.make_async_copy(sent, sent, x_send.at[kind]).wait()
        pltpu.make_async_copy(ref, ref, x_recv.at[kind]).wait()


def grad_kernel(me_ref, h_ref, g_ref, act_ref, du_ref, win_ref, gain_ref, din, dout, dgain):
    raw = jnp.dot(h_ref[...].T, du_ref[...], preferred_element_type=jnp.float32)
    rows = raw.shape[0]
    gain = jnp.broadcast_to(gain_ref[...], (128, rows)).T[:, :1]
    din[...] = raw * gain
    sums = jnp.sum(win_ref[...].astype(jnp.float32) * raw, axis=1, keepdims=True)
    dgain[...] = jnp.broadcast_to(sums, (rows, 128)).T[:1]
    dout[...] = jnp.dot(g_ref[...].T, act_ref[...], preferred_element_type=jnp.float32)


def gradients(me, h, g, act, du, weight_in, gains):
    total, block = h.shape
    hidden = act.shape[1]
    rows = min(256, block)
    steps = block // rows
    tall = pl.BlockSpec((total, rows), lambda i, me_ref: (0, i))
    whole = pl.BlockSpec((total, hidden), lambda i, me_ref: (0, 0))
    out = pl.BlockSpec((rows, hidden), lambda i, me_ref: (i, 0))
    return pl.pallas_call(
        grad_kernel,
        grid_spec=pltpu.PrefetchScalarGridSpec(
            num_scalar_prefetch=1,
            grid=(steps,),
            in_specs=[
                tall,
                tall,
                whole,
                whole,
                pl.BlockSpec((rows, hidden), lambda i, me_ref: (me_ref[0] * steps + i, 0)),
                pl.BlockSpec((1, rows), lambda i, me_ref: (0, me_ref[0] * steps + i)),
            ],
            out_specs=[out, out, pl.BlockSpec((1, rows), lambda i, me_ref: (0, i))],
        ),
        out_shape=(
            jax.ShapeDtypeStruct((block, hidden), jnp.float32),
            jax.ShapeDtypeStruct((block, hidden), jnp.float32),
            jax.ShapeDtypeStruct((1, block), jnp.float32),
        ),
        compiler_params=pltpu.CompilerParams(vmem_limit_bytes=32 * 2**20),
    )(me, h, g, act, du, weight_in, gains)


def local(sections, replicas, inputs, cotangent, weight_in, weight_out, norm_gains):
    tokens, width = inputs.shape
    hidden = weight_in.shape[2]
    micros = tokens // ROWS
    block = width // replicas
    wide = jax.ShapeDtypeStruct((replicas, micros, ROWS, block), jnp.bfloat16)
    narrow = jax.ShapeDtypeStruct((replicas, micros, ROWS, hidden), jnp.bfloat16)
    any_spec = pl.BlockSpec(memory_space=pl.ANY)
    vmem_spec = pl.BlockSpec(memory_space=pltpu.VMEM)
    wide_scratch = pltpu.VMEM((micros, ROWS, width), jnp.bfloat16)
    weight_scratch = pltpu.VMEM((width, hidden), jnp.bfloat16)
    flipped_scratch = pltpu.VMEM((hidden, width), jnp.bfloat16)
    dma = pltpu.SemaphoreType.DMA
    all_h, all_g, all_act, all_du = pl.pallas_call(
        functools.partial(relay_kernel, sections, replicas, micros),
        out_shape=(wide, wide, narrow, narrow),
        in_specs=[any_spec] * 4 + [vmem_spec],
        out_specs=(any_spec,) * 4,
        scratch_shapes=[
            weight_scratch,
            weight_scratch,
            flipped_scratch,
            flipped_scratch,
            wide_scratch,
            wide_scratch,
            wide_scratch,
            wide_scratch,
            pltpu.VMEM((micros, ROWS, hidden), jnp.bfloat16),
            pltpu.VMEM((micros, ROWS, hidden), jnp.bfloat16),
            pltpu.VMEM((micros, ROWS, hidden), jnp.float32),
            pltpu.VMEM((micros, ROWS, 128), jnp.float32),
            dma((2, width // WCHUNK)),
            dma((micros, 3)),
            dma((micros, 3)),
            dma((micros, 3)),
            dma((micros, 3)),
            dma((4,)),
            dma((4,)),
        ],
        compiler_params=pltpu.CompilerParams(
            collective_id=0, has_side_effects=True, vmem_limit_bytes=62 * 2**20
        ),
    )(
        inputs.reshape(micros, ROWS, width),
        cotangent.reshape(micros, ROWS, width),
        weight_in[0],
        weight_out[0],
        norm_gains,
    )
    total = replicas * tokens
    me = lax.axis_index("dp").astype(jnp.int32).reshape(1)
    in_grad, out_grad, gain_grad = gradients(
        me,
        all_h.reshape(total, block),
        all_g.reshape(total, block),
        all_act.reshape(total, hidden),
        all_du.reshape(total, hidden),
        weight_in[0],
        norm_gains,
    )
    return (in_grad[None], out_grad[None], gain_grad)


def solution(mesh):
    return jax.shard_map(
        functools.partial(local, mesh.shape["section"], mesh.shape["dp"]),
        mesh=mesh,
        in_specs=(
            P("dp", None),
            P("dp", None),
            P("section", None, None),
            P("section", None, None),
            P("section", None),
        ),
        out_specs=(P("section", "dp", None), P("section", "dp", None), P("section", "dp")),
        check_vma=False,
    )
```

```python
import functools

import jax
import jax.numpy as jnp
from jax import lax
from jax.experimental import pallas as pl
from jax.experimental.pallas import tpu as pltpu
from jax.sharding import PartitionSpec as P

ROWS = 16
LAG = 10
EPSILON = 1e-05
MESH = pl.DeviceIdType.MESH


def dot(left, right):
    return jnp.dot(left, right, preferred_element_type=jnp.float32)


def nt_dot(left, right):
    return lax.dot_general(
        left, right, (((1,), (1,)), ((), ())), preferred_element_type=jnp.float32
    )


def relay_kernel(
    sections,
    replicas,
    micros,
    x_ref,
    c_ref,
    win_hbm,
    wout_hbm,
    gain_ref,
    all_h,
    all_g,
    all_act,
    all_du,
    win,
    wout,
    win_t,
    wout_t,
    gain,
    stash,
    up,
    out_f,
    out_b,
    act_buf,
    du_buf,
    pre,
    scale,
    fx_send,
    fx_recv,
    bx_send,
    bx_recv,
    w_sem,
    f_recv,
    b_recv,
    f_send,
    b_send,
    fx_sem,
    bx_sem,
    xs_sem,
    x_recv,
    x_send,
):
    half = stash.shape[2]
    width = 2 * half
    hidden = win.shape[1]
    count = 2 * micros
    block = width // replicas
    chips = replicas // 2
    quarter = half // 4
    pieces = ((0, quarter), (quarter, 2 * quarter), (3 * quarter, quarter))
    take = ((0, 3),)
    give = ((0, 3),)
    piece_of = [
        [k for k, (start, size) in enumerate(pieces) if start <= j * block < start + size][0]
        for j in range(chips)
    ]
    pos = lax.axis_index("section")
    me = lax.axis_index("dp")
    chip = me // 2
    core = lax.rem(me, 2)
    partner = me + 1 - 2 * core
    is_first = pos == 0
    is_last = pos == sections - 1
    not_first = pos > 0
    not_last = pos < sections - 1

    def part(owner):
        return pl.ds(pl.multiple_of(owner * block, block), block)

    def mine(j):
        return slice(j * block, (j + 1) * block)

    def span(first, past):
        start = pieces[first][0]
        return start, pieces[past - 1][0] + pieces[past - 1][1]

    def wcopy(kind, j):
        src, dst = ((win_hbm, win), (wout_hbm, wout))[kind]
        return pltpu.make_async_copy(
            src.at[part(2 * j + core), :], dst.at[mine(j), :], w_sem.at[kind, j]
        )

    def load_weights(kind):
        for j in range(chips):
            wcopy(kind, j).start()

    def load_own(src, dst, sems, m):
        for j in range(chips):
            pltpu.make_async_copy(
                src.at[m, :, part(2 * j + core)],
                dst.at[2 * m + core, :, mine(j)],
                sems.at[2 * m + core, piece_of[j]],
            ).start()

    def push_partner(src, dst, sems, m):
        for j in range(chips):
            pltpu.make_async_remote_copy(
                src_ref=src.at[m, :, part(2 * j + 1 - core)],
                dst_ref=dst.at[2 * m + core, :, mine(j)],
                send_sem=xs_sem.at[0],
                recv_sem=sems.at[2 * m + core, piece_of[j]],
                device_id={"dp": partner},
                device_id_type=MESH,
            ).start()

    def spread(src, dst, kind):
        @pl.loop(1, replicas)
        def _(step):
            peer = lax.rem(me + step, replicas)
            pltpu.make_async_remote_copy(
                src_ref=src.at[:, :, part(peer)],
                dst_ref=dst.at[me],
                send_sem=x_send.at[kind],
                recv_sem=x_recv.at[kind],
                device_id={"dp": peer},
                device_id_type=MESH,
            ).start()

    @pl.when(is_first)
    def _():
        load_own(x_ref, stash, f_recv, 0)
        load_weights(0)
        load_weights(1)

        @pl.loop(1, micros)
        def _(m):
            load_own(x_ref, stash, f_recv, m)

    @pl.when(not_first)
    def _():
        load_weights(1)
        load_weights(0)

    @pl.when(is_last)
    def _():
        @pl.loop(0, micros)
        def _(m):
            load_own(c_ref, up, b_recv, m)

    barrier = pltpu.get_barrier_semaphore()

    @pl.when(not_first)
    def _():
        pl.semaphore_signal(
            barrier, inc=1, device_id={"section": pos - 1}, device_id_type=MESH
        )

    @pl.when(not_last)
    def _():
        pl.semaphore_signal(
            barrier, inc=1, device_id={"section": pos + 1}, device_id_type=MESH
        )

    @pl.loop(1, replicas)
    def _(step):
        pl.semaphore_signal(
            barrier,
            inc=1,
            device_id={"dp": lax.rem(me + step, replicas)},
            device_id_type=MESH,
        )

    for j in range(chips):
        gain[:, mine(j)] = gain_ref[:, part(2 * j + core)]

    pl.semaphore_wait(
        barrier,
        replicas - 1 + not_first.astype(jnp.int32) + not_last.astype(jnp.int32),
    )

    @pl.when(is_first)
    def _():
        @pl.loop(0, micros)
        def _(m):
            push_partner(x_ref, stash, f_recv, m)

        spread(x_ref, all_h, 0)

    @pl.when(is_last)
    def _():
        @pl.loop(0, micros)
        def _(m):
            push_partner(c_ref, up, b_recv, m)

        spread(c_ref, all_g, 2)

    @pl.when(not_first)
    def _():
        for j in range(chips):
            wcopy(1, j).wait()

            @pl.when(not_last)
            def _():
                wout_t[:, mine(j)] = wout[mine(j), :].T

        for j in range(chips):
            wcopy(0, j).wait()
            win_t[:, mine(j)] = win[mine(j), :].T

    def send_forward(i, k):
        start, size = pieces[k]
        return pltpu.make_async_remote_copy(
            src_ref=out_f.at[i, :, pl.ds(start, size)],
            dst_ref=stash.at[i, :, pl.ds(start, size)],
            send_sem=f_send.at[i, k],
            recv_sem=f_recv.at[i, k],
            device_id={"section": pos + 1},
            device_id_type=MESH,
        )

    def send_backward(i, k):
        start, size = pieces[k]
        return pltpu.make_async_remote_copy(
            src_ref=out_b.at[i, :, pl.ds(start, size)],
            dst_ref=up.at[i, :, pl.ds(start, size)],
            send_sem=b_send.at[i, k],
            recv_sem=b_recv.at[i, k],
            device_id={"section": pos - 1},
            device_id_type=MESH,
        )

    def trade_forward(i):
        return pltpu.make_async_remote_copy(
            src_ref=fx_send.at[i],
            dst_ref=fx_recv.at[i],
            send_sem=xs_sem.at[1],
            recv_sem=fx_sem.at[i],
            device_id={"dp": partner},
            device_id_type=MESH,
        )

    def trade_backward(i):
        return pltpu.make_async_remote_copy(
            src_ref=bx_send.at[i],
            dst_ref=bx_recv.at[i],
            send_sem=xs_sem.at[2],
            recv_sem=bx_sem.at[i],
            device_id={"dp": partner},
            device_id_type=MESH,
        )

    def arrived(buffer, sems, i, first, past):
        for k in range(first, past):
            start, size = pieces[k]
            piece = buffer.at[i, :, pl.ds(start, size)]
            pltpu.make_async_copy(piece, piece, sems.at[i, k]).wait()

    def share(kind, i, src_of, dst):
        slot = dst.at[2 * chip + lax.rem(i, 2), i // 2]
        pltpu.make_async_copy(src_of(chip), slot, x_recv.at[kind]).start()
        for step in range(1, chips):
            target = lax.rem(chip + step, chips)
            pltpu.make_async_remote_copy(
                src_ref=src_of(target),
                dst_ref=slot,
                send_sem=x_send.at[kind],
                recv_sem=x_recv.at[kind],
                device_id={"dp": 2 * target + core},
                device_id_type=MESH,
            ).start()

    def keep_own(kind, i, src, dst):
        @pl.when(lax.rem(i, 2) == core)
        def _():
            pltpu.make_async_copy(
                src.at[i, :, part(chip)], dst.at[me, i // 2], x_recv.at[kind]
            ).start()

    def forward_in(i):
        total = jnp.zeros((ROWS, 1), jnp.float32)
        u = jnp.zeros((ROWS, hidden), jnp.float32)
        for first, past in take:
            start, stop = span(first, past)
            arrived(stash, f_recv, i, first, past)

            @pl.when((i == 0) & is_first)
            def _():
                for j in range(chips):
                    if start <= j * block < stop:
                        wcopy(0, j).wait()

            h = stash[i, :, start:stop].astype(jnp.float32)
            scaled = (h * gain[:, start:stop]).astype(jnp.bfloat16)
            total = total + jnp.sum(h * h, axis=1, keepdims=True)
            u = u + dot(scaled, win[start:stop, :])
        fx_send[i, :, :hidden] = u
        fx_send[i, :, hidden:] = jnp.broadcast_to(total, (ROWS, 128))
        trade_forward(i).start()

        @pl.when(is_first)
        def _():
            keep_own(0, i, stash, all_h)

        @pl.when(not_first)
        def _():
            share(0, i, lambda j: stash.at[i, :, part(j)], all_h)

    def forward_out(i):
        pltpu.make_async_copy(fx_recv.at[i], fx_recv.at[i], fx_sem.at[i]).wait()
        total = fx_send[i, :, hidden:] + fx_recv[i, :, hidden:]
        inv = lax.rsqrt(total / width + EPSILON)
        scale[i] = inv
        u = (fx_send[i, :, :hidden] + fx_recv[i, :, :hidden]) * inv[:, :1]
        act = (u * jax.nn.sigmoid(u)).astype(jnp.bfloat16)
        pre[i] = u
        act_buf[i] = act

        @pl.when((i == 0) & is_first)
        def _():
            for j in range(chips):
                wcopy(1, j).wait()

        def emit(product):
            for first, past in give:
                start, stop = span(first, past)
                h = stash[i, :, start:stop].astype(jnp.float32)
                out_f[i, :, start:stop] = (h + product(act, start, stop)).astype(
                    jnp.bfloat16
                )
                for k in range(first, past):
                    send_forward(i, k).start()

        @pl.when(is_first)
        def _():
            emit(lambda a, start, stop: nt_dot(a, wout[start:stop, :]))

        @pl.when(not_first & not_last)
        def _():
            emit(lambda a, start, stop: dot(a, wout_t[:, start:stop]))

        share(1, i, lambda j: act_buf.at[i], all_act)

    def backward_in(i):
        da = jnp.zeros((ROWS, hidden), jnp.float32)
        for first, past in take:
            start, stop = span(first, past)
            arrived(up, b_recv, i, first, past)
            da = da + dot(up[i, :, start:stop], wout[start:stop, :])
        bx_send[i] = da
        trade_backward(i).start()

        @pl.when(is_last)
        def _():
            keep_own(2, i, up, all_g)

        @pl.when(not_last)
        def _():
            share(2, i, lambda j: up.at[i, :, part(j)], all_g)

    def backward_out(i):
        pltpu.make_async_copy(bx_recv.at[i], bx_recv.at[i], bx_sem.at[i]).wait()
        da = bx_send[i] + bx_recv[i]
        u = pre[i]
        inv = scale[i][:, :1]
        sig = jax.nn.sigmoid(u)
        wide_du = da * sig * (1.0 + u * (1.0 - sig))
        du = wide_du.astype(jnp.bfloat16)
        du_buf[i] = (wide_du * inv).astype(jnp.bfloat16)

        @pl.when(not_first)
        def _():
            centered = jnp.sum(du.astype(jnp.float32) * u, axis=1, keepdims=True) / (
                inv * width
            )
            pull = inv * inv * inv * centered
            for first, past in give:
                start, stop = span(first, past)
                h = stash[i, :, start:stop].astype(jnp.float32)
                g = up[i, :, start:stop].astype(jnp.float32)
                dn = dot(du, win_t[:, start:stop])
                out_b[i, :, start:stop] = (
                    g + inv * (dn * gain[:, start:stop]) - h * pull
                ).astype(jnp.bfloat16)
                for k in range(first, past):
                    send_backward(i, k).start()

        share(3, i, lambda j: du_buf.at[i], all_du)

    lag = jnp.minimum(LAG * (sections - 1 - pos) // 2, count)
    lead = is_first.astype(jnp.int32)

    @pl.loop(0, count + lag + lead)
    def _(step):
        ahead = step - lead
        back = step - lag

        @pl.when(step < count)
        def _():
            forward_in(step)

        @pl.when((back >= 0) & (back < count))
        def _():
            backward_in(back)

        @pl.when((ahead >= 0) & (ahead < count))
        def _():
            forward_out(ahead)

        @pl.when((back >= 0) & (back < count))
        def _():
            backward_out(back)

    @pl.loop(0, count)
    def _(i):
        for k in range(len(pieces)):

            @pl.when(not_last)
            def _():
                send_forward(i, k).wait_send()

            @pl.when(not_first)
            def _():
                send_backward(i, k).wait_send()

    def drain(ref, sem):
        pltpu.make_async_copy(ref, ref, sem).wait()

    @pl.when(is_first | is_last)
    def _():
        drain(stash.at[pl.ds(0, micros)], xs_sem.at[0])

    drain(fx_send, xs_sem.at[1])
    drain(bx_send, xs_sem.at[2])
    for kind, ref, early in (
        (0, all_h, is_first),
        (1, all_act, False),
        (2, all_g, is_last),
        (3, all_du, False),
    ):
        drain(ref.at[pl.ds(0, replicas - 2)], x_send.at[kind])
        if early is not False:

            @pl.when(early)
            def _():
                drain(ref.at[0], x_send.at[kind])

        drain(ref, x_recv.at[kind])


def grad_kernel(me_ref, h_ref, g_ref, act_ref, du_ref, win_ref, gain_ref, din, dout, dgain):
    raw = jnp.dot(h_ref[...].T, du_ref[...], preferred_element_type=jnp.float32)
    rows = raw.shape[0]
    gain = jnp.broadcast_to(gain_ref[...], (128, rows)).T[:, :1]
    din[...] = raw * gain
    sums = jnp.sum(win_ref[...].astype(jnp.float32) * raw, axis=1, keepdims=True)
    dgain[...] = jnp.broadcast_to(sums, (rows, 128)).T[:1]
    dout[...] = jnp.dot(g_ref[...].T, act_ref[...], preferred_element_type=jnp.float32)


def gradients(me, h, g, act, du, weight_in, gains):
    total, block = h.shape
    hidden = act.shape[1]
    rows = min(256, block)
    steps = block // rows
    tall = pl.BlockSpec((total, rows), lambda i, me_ref: (0, i))
    whole = pl.BlockSpec((total, hidden), lambda i, me_ref: (0, 0))
    out = pl.BlockSpec((rows, hidden), lambda i, me_ref: (i, 0))
    return pl.pallas_call(
        grad_kernel,
        grid_spec=pltpu.PrefetchScalarGridSpec(
            num_scalar_prefetch=1,
            grid=(steps,),
            in_specs=[
                tall,
                tall,
                whole,
                whole,
                pl.BlockSpec((rows, hidden), lambda i, me_ref: (me_ref[0] * steps + i, 0)),
                pl.BlockSpec((1, rows), lambda i, me_ref: (0, me_ref[0] * steps + i)),
            ],
            out_specs=[out, out, pl.BlockSpec((1, rows), lambda i, me_ref: (0, i))],
        ),
        out_shape=(
            jax.ShapeDtypeStruct((block, hidden), jnp.float32),
            jax.ShapeDtypeStruct((block, hidden), jnp.float32),
            jax.ShapeDtypeStruct((1, block), jnp.float32),
        ),
        compiler_params=pltpu.CompilerParams(vmem_limit_bytes=62 * 2**20),
    )(me, h, g, act, du, weight_in, gains)


def local(sections, replicas, inputs, cotangent, weight_in, weight_out, norm_gains):
    tokens, width = inputs.shape
    hidden = weight_in.shape[2]
    micros = tokens // ROWS
    count = 2 * micros
    block = width // replicas
    half = width // 2
    wide = jax.ShapeDtypeStruct((replicas, micros, ROWS, block), jnp.bfloat16)
    narrow = jax.ShapeDtypeStruct((replicas, micros, ROWS, hidden), jnp.bfloat16)
    any_spec = pl.BlockSpec(memory_space=pl.ANY)
    vmem_spec = pl.BlockSpec(memory_space=pltpu.VMEM)
    wide_scratch = pltpu.VMEM((count, ROWS, half), jnp.bfloat16)
    narrow_scratch = pltpu.VMEM((count, ROWS, hidden), jnp.bfloat16)
    sums_scratch = pltpu.VMEM((count, ROWS, hidden + 128), jnp.float32)
    rows_scratch = pltpu.VMEM((count, ROWS, hidden), jnp.float32)
    dma = pltpu.SemaphoreType.DMA
    all_h, all_g, all_act, all_du = pl.pallas_call(
        functools.partial(relay_kernel, sections, replicas, micros),
        out_shape=(wide, wide, narrow, narrow),
        in_specs=[any_spec] * 4 + [vmem_spec],
        out_specs=(any_spec,) * 4,
        scratch_shapes=[
            pltpu.VMEM((half, hidden), jnp.bfloat16),
            pltpu.VMEM((half, hidden), jnp.bfloat16),
            pltpu.VMEM((hidden, half), jnp.bfloat16),
            pltpu.VMEM((hidden, half), jnp.bfloat16),
            pltpu.VMEM((1, half), jnp.float32),
            wide_scratch,
            wide_scratch,
            wide_scratch,
            wide_scratch,
            narrow_scratch,
            narrow_scratch,
            rows_scratch,
            pltpu.VMEM((count, ROWS, 128), jnp.float32),
            sums_scratch,
            sums_scratch,
            rows_scratch,
            rows_scratch,
            dma((2, replicas // 2)),
            dma((count, 3)),
            dma((count, 3)),
            dma((count, 3)),
            dma((count, 3)),
            dma((count,)),
            dma((count,)),
            dma((3,)),
            dma((4,)),
            dma((4,)),
        ],
        compiler_params=pltpu.CompilerParams(
            collective_id=0, has_side_effects=True, vmem_limit_bytes=62 * 2**20
        ),
    )(
        inputs.reshape(micros, ROWS, width),
        cotangent.reshape(micros, ROWS, width),
        weight_in[0],
        weight_out[0],
        norm_gains,
    )
    total = replicas * tokens
    me = lax.axis_index("dp").astype(jnp.int32).reshape(1)
    in_grad, out_grad, gain_grad = gradients(
        me,
        all_h.reshape(total, block),
        all_g.reshape(total, block),
        all_act.reshape(total, hidden),
        all_du.reshape(total, hidden),
        weight_in[0],
        norm_gains,
    )
    return (in_grad[None], out_grad[None], gain_grad)


def solution(mesh):
    return jax.shard_map(
        functools.partial(local, mesh.shape["section"], mesh.shape["dp"]),
        mesh=mesh,
        in_specs=(
            P("dp", None),
            P("dp", None),
            P("section", None, None),
            P("section", None, None),
            P("section", None),
        ),
        out_specs=(P("section", "dp", None), P("section", "dp", None), P("section", "dp")),
        check_vma=False,
    )
```

```python
import functools

import jax
import jax.numpy as jnp
from jax import lax
from jax.experimental import pallas as pl
from jax.experimental.pallas import tpu as pltpu
from jax.sharding import PartitionSpec as P

ROWS = 16
LAG = 11
LAST_FINE = 2
EPSILON = 1e-05
MESH = pl.DeviceIdType.MESH


def dot(left, right):
    return jnp.dot(left, right, preferred_element_type=jnp.float32)


def nt_dot(left, right):
    return lax.dot_general(
        left, right, (((1,), (1,)), ((), ())), preferred_element_type=jnp.float32
    )


def relay_kernel(
    sections,
    replicas,
    micros,
    x_ref,
    c_ref,
    win_hbm,
    wout_hbm,
    gain_ref,
    all_h,
    all_g,
    all_act,
    all_du,
    win,
    wout,
    win_t,
    wout_t,
    gain,
    stash,
    up,
    out_f,
    out_b,
    act_buf,
    du_buf,
    pre,
    scale,
    fx_send,
    fx_recv,
    bx_send,
    bx_recv,
    w_sem,
    f_recv,
    b_recv,
    f_send,
    b_send,
    fx_sem,
    bx_sem,
    xs_sem,
    x_recv,
    x_send,
):
    half = stash.shape[2]
    width = 2 * half
    hidden = win.shape[1]
    count = 2 * micros
    block = width // replicas
    chips = replicas // 2
    quarter = half // 4
    pieces = ((0, quarter), (quarter, 2 * quarter), (3 * quarter, quarter))
    take = {True: ((0, 2), (2, 3)), False: ((0, 3),)}
    give = {True: ((0, 1), (1, 3)), False: ((0, 3),)}
    piece_of = [
        [k for k, (start, size) in enumerate(pieces) if start <= j * block < start + size][0]
        for j in range(chips)
    ]
    pos = lax.axis_index("section")
    me = lax.axis_index("dp")
    chip = me // 2
    core = lax.rem(me, 2)
    partner = me + 1 - 2 * core
    is_first = pos == 0
    is_last = pos == sections - 1
    not_first = pos > 0
    not_last = pos < sections - 1

    def part(owner):
        return pl.ds(pl.multiple_of(owner * block, block), block)

    def mine(j):
        return slice(j * block, (j + 1) * block)

    def span(first, past):
        start = pieces[first][0]
        return start, pieces[past - 1][0] + pieces[past - 1][1]

    def wcopy(kind, j):
        src, dst = ((win_hbm, win), (wout_hbm, wout))[kind]
        return pltpu.make_async_copy(
            src.at[part(2 * j + core), :], dst.at[mine(j), :], w_sem.at[kind, j]
        )

    def load_weights(kind):
        for j in range(chips):
            wcopy(kind, j).start()

    def load_own(src, dst, sems, m):
        for j in range(chips):
            pltpu.make_async_copy(
                src.at[m, :, part(2 * j + core)],
                dst.at[2 * m + core, :, mine(j)],
                sems.at[2 * m + core, piece_of[j]],
            ).start()

    def push_partner(src, dst, sems, m):
        for j in range(chips):
            pltpu.make_async_remote_copy(
                src_ref=src.at[m, :, part(2 * j + 1 - core)],
                dst_ref=dst.at[2 * m + core, :, mine(j)],
                send_sem=xs_sem.at[0],
                recv_sem=sems.at[2 * m + core, piece_of[j]],
                device_id={"dp": partner},
                device_id_type=MESH,
            ).start()

    def spread(src, dst, kind):
        @pl.loop(1, replicas)
        def _(step):
            peer = lax.rem(me + step, replicas)
            pltpu.make_async_remote_copy(
                src_ref=src.at[:, :, part(peer)],
                dst_ref=dst.at[me],
                send_sem=x_send.at[kind],
                recv_sem=x_recv.at[kind],
                device_id={"dp": peer},
                device_id_type=MESH,
            ).start()

    @pl.when(is_first)
    def _():
        load_own(x_ref, stash, f_recv, 0)
        load_weights(0)
        load_weights(1)

        @pl.loop(1, micros)
        def _(m):
            load_own(x_ref, stash, f_recv, m)

    @pl.when(not_first)
    def _():
        load_weights(1)
        load_weights(0)

    @pl.when(is_last)
    def _():
        @pl.loop(0, micros)
        def _(m):
            load_own(c_ref, up, b_recv, m)

    barrier = pltpu.get_barrier_semaphore()

    @pl.when(not_first)
    def _():
        pl.semaphore_signal(
            barrier, inc=1, device_id={"section": pos - 1}, device_id_type=MESH
        )

    @pl.when(not_last)
    def _():
        pl.semaphore_signal(
            barrier, inc=1, device_id={"section": pos + 1}, device_id_type=MESH
        )

    @pl.loop(1, replicas)
    def _(step):
        pl.semaphore_signal(
            barrier,
            inc=1,
            device_id={"dp": lax.rem(me + step, replicas)},
            device_id_type=MESH,
        )

    for j in range(chips):
        gain[:, mine(j)] = gain_ref[:, part(2 * j + core)]

    pl.semaphore_wait(
        barrier,
        replicas - 1 + not_first.astype(jnp.int32) + not_last.astype(jnp.int32),
    )

    @pl.when(is_first)
    def _():
        @pl.loop(0, micros)
        def _(m):
            push_partner(x_ref, stash, f_recv, m)

        spread(x_ref, all_h, 0)

    @pl.when(is_last)
    def _():
        @pl.loop(0, micros)
        def _(m):
            push_partner(c_ref, up, b_recv, m)

        spread(c_ref, all_g, 2)

    @pl.when(not_first)
    def _():
        for j in range(chips):
            wcopy(1, j).wait()

            @pl.when(not_last)
            def _():
                wout_t[:, mine(j)] = wout[mine(j), :].T

        for j in range(chips):
            wcopy(0, j).wait()
            win_t[:, mine(j)] = win[mine(j), :].T

    def send_forward(i, k):
        start, size = pieces[k]
        return pltpu.make_async_remote_copy(
            src_ref=out_f.at[i, :, pl.ds(start, size)],
            dst_ref=stash.at[i, :, pl.ds(start, size)],
            send_sem=f_send.at[i, k],
            recv_sem=f_recv.at[i, k],
            device_id={"section": pos + 1},
            device_id_type=MESH,
        )

    def send_backward(i, k):
        start, size = pieces[k]
        return pltpu.make_async_remote_copy(
            src_ref=out_b.at[i, :, pl.ds(start, size)],
            dst_ref=up.at[i, :, pl.ds(start, size)],
            send_sem=b_send.at[i, k],
            recv_sem=b_recv.at[i, k],
            device_id={"section": pos - 1},
            device_id_type=MESH,
        )

    def trade_forward(i):
        return pltpu.make_async_remote_copy(
            src_ref=fx_send.at[i],
            dst_ref=fx_recv.at[i],
            send_sem=xs_sem.at[1],
            recv_sem=fx_sem.at[i],
            device_id={"dp": partner},
            device_id_type=MESH,
        )

    def trade_backward(i):
        return pltpu.make_async_remote_copy(
            src_ref=bx_send.at[i],
            dst_ref=bx_recv.at[i],
            send_sem=xs_sem.at[2],
            recv_sem=bx_sem.at[i],
            device_id={"dp": partner},
            device_id_type=MESH,
        )

    def arrived(buffer, sems, i, first, past):
        for k in range(first, past):
            start, size = pieces[k]
            piece = buffer.at[i, :, pl.ds(start, size)]
            pltpu.make_async_copy(piece, piece, sems.at[i, k]).wait()

    def share(kind, i, src_of, dst):
        slot = dst.at[2 * chip + lax.rem(i, 2), i // 2]
        pltpu.make_async_copy(src_of(chip), slot, x_recv.at[kind]).start()
        for step in range(1, chips):
            target = lax.rem(chip + step, chips)
            pltpu.make_async_remote_copy(
                src_ref=src_of(target),
                dst_ref=slot,
                send_sem=x_send.at[kind],
                recv_sem=x_recv.at[kind],
                device_id={"dp": 2 * target + core},
                device_id_type=MESH,
            ).start()

    def keep_own(kind, i, src, dst):
        @pl.when(lax.rem(i, 2) == core)
        def _():
            pltpu.make_async_copy(
                src.at[i, :, part(chip)], dst.at[me, i // 2], x_recv.at[kind]
            ).start()

    def forward_in(i, fine):
        total = jnp.zeros((ROWS, 1), jnp.float32)
        u = jnp.zeros((ROWS, hidden), jnp.float32)
        for first, past in take[fine]:
            start, stop = span(first, past)
            arrived(stash, f_recv, i, first, past)

            if fine:

                @pl.when((i == 0) & is_first)
                def _():
                    for j in range(chips):
                        if start <= j * block < stop:
                            wcopy(0, j).wait()

            h = stash[i, :, start:stop].astype(jnp.float32)
            scaled = (h * gain[:, start:stop]).astype(jnp.bfloat16)
            total = total + jnp.sum(h * h, axis=1, keepdims=True)
            u = u + dot(scaled, win[start:stop, :])
        fx_send[i, :, :hidden] = u
        fx_send[i, :, hidden:] = jnp.broadcast_to(total, (ROWS, 128))
        trade_forward(i).start()

        @pl.when(is_first)
        def _():
            keep_own(0, i, stash, all_h)

        @pl.when(not_first)
        def _():
            share(0, i, lambda j: stash.at[i, :, part(j)], all_h)

    def forward_out(i, fine):
        pltpu.make_async_copy(fx_recv.at[i], fx_recv.at[i], fx_sem.at[i]).wait()
        total = fx_send[i, :, hidden:] + fx_recv[i, :, hidden:]
        inv = lax.rsqrt(total / width + EPSILON)
        scale[i] = inv
        u = (fx_send[i, :, :hidden] + fx_recv[i, :, :hidden]) * inv[:, :1]
        act = (u * jax.nn.sigmoid(u)).astype(jnp.bfloat16)
        pre[i] = u
        act_buf[i] = act

        if fine:

            @pl.when((i == 0) & is_first)
            def _():
                for j in range(chips):
                    wcopy(1, j).wait()

        def emit(product):
            for first, past in give[fine]:
                start, stop = span(first, past)
                h = stash[i, :, start:stop].astype(jnp.float32)
                out_f[i, :, start:stop] = (h + product(act, start, stop)).astype(
                    jnp.bfloat16
                )
                for k in range(first, past):
                    send_forward(i, k).start()

        if fine:

            @pl.when(is_first)
            def _():
                emit(lambda a, start, stop: nt_dot(a, wout[start:stop, :]))

        @pl.when(not_first & not_last)
        def _():
            emit(lambda a, start, stop: dot(a, wout_t[:, start:stop]))

        share(1, i, lambda j: act_buf.at[i], all_act)

    def backward_in(i, fine):
        da = jnp.zeros((ROWS, hidden), jnp.float32)
        for first, past in take[fine]:
            start, stop = span(first, past)
            arrived(up, b_recv, i, first, past)
            da = da + dot(up[i, :, start:stop], wout[start:stop, :])
        bx_send[i] = da
        trade_backward(i).start()

        @pl.when(is_last)
        def _():
            keep_own(2, i, up, all_g)

        @pl.when(not_last)
        def _():
            share(2, i, lambda j: up.at[i, :, part(j)], all_g)

    def backward_out(i, fine):
        pltpu.make_async_copy(bx_recv.at[i], bx_recv.at[i], bx_sem.at[i]).wait()
        da = bx_send[i] + bx_recv[i]
        u = pre[i]
        inv = scale[i][:, :1]
        sig = jax.nn.sigmoid(u)
        wide_du = da * sig * (1.0 + u * (1.0 - sig))
        du = wide_du.astype(jnp.bfloat16)
        du_buf[i] = (wide_du * inv).astype(jnp.bfloat16)

        @pl.when(not_first)
        def _():
            centered = jnp.sum(du.astype(jnp.float32) * u, axis=1, keepdims=True) / (
                inv * width
            )
            pull = inv * inv * inv * centered
            for first, past in give[fine]:
                start, stop = span(first, past)
                h = stash[i, :, start:stop].astype(jnp.float32)
                g = up[i, :, start:stop].astype(jnp.float32)
                dn = dot(du, win_t[:, start:stop])
                out_b[i, :, start:stop] = (
                    g + inv * (dn * gain[:, start:stop]) - h * pull
                ).astype(jnp.bfloat16)
                for k in range(first, past):
                    send_backward(i, k).start()

        share(3, i, lambda j: du_buf.at[i], all_du)

    lag = jnp.minimum(LAG * (sections - 1 - pos) // 2, count)
    lag = jnp.where(is_first, count, lag)
    lead = is_first.astype(jnp.int32)

    @pl.loop(0, count + lag)
    def _(step):
        ahead = step - lead
        back = step - lag
        both = (back >= 0) & (step < count)
        last = (step >= count) & (back >= count - LAST_FINE)

        @pl.when(both)
        def _():
            forward_in(step, False)
            backward_in(back, False)
            forward_out(step, False)
            backward_out(back, False)

        @pl.when((step < count) & (back < 0))
        def _():
            forward_in(step, True)

        @pl.when((ahead >= 0) & (ahead < count) & (ahead < lag))
        def _():
            forward_out(ahead, True)

        @pl.when((step >= count) & jnp.logical_not(last))
        def _():
            backward_in(back, False)
            backward_out(back, False)

        @pl.when(last)
        def _():
            backward_in(back, True)
            backward_out(back, True)

    @pl.loop(0, count)
    def _(i):
        for k in range(len(pieces)):

            @pl.when(not_last)
            def _():
                send_forward(i, k).wait_send()

            @pl.when(not_first)
            def _():
                send_backward(i, k).wait_send()

    def drain(ref, sem):
        pltpu.make_async_copy(ref, ref, sem).wait()

    @pl.when(is_first | is_last)
    def _():
        drain(stash.at[pl.ds(0, micros)], xs_sem.at[0])

    drain(fx_send, xs_sem.at[1])
    drain(bx_send, xs_sem.at[2])
    for kind, ref, early in (
        (0, all_h, is_first),
        (1, all_act, False),
        (2, all_g, is_last),
        (3, all_du, False),
    ):
        drain(ref.at[pl.ds(0, replicas - 2)], x_send.at[kind])
        if early is not False:

            @pl.when(early)
            def _():
                drain(ref.at[0], x_send.at[kind])

        drain(ref, x_recv.at[kind])


def grad_kernel(me_ref, h_ref, g_ref, act_ref, du_ref, win_ref, gain_ref, din, dout, dgain):
    raw = jnp.dot(h_ref[...].T, du_ref[...], preferred_element_type=jnp.float32)
    rows = raw.shape[0]
    gain = jnp.broadcast_to(gain_ref[...], (128, rows)).T[:, :1]
    din[...] = raw * gain
    sums = jnp.sum(win_ref[...].astype(jnp.float32) * raw, axis=1, keepdims=True)
    dgain[...] = jnp.broadcast_to(sums, (rows, 128)).T[:1]
    dout[...] = jnp.dot(g_ref[...].T, act_ref[...], preferred_element_type=jnp.float32)


def gradients(me, h, g, act, du, weight_in, gains):
    total, block = h.shape
    hidden = act.shape[1]
    rows = min(256, block)
    steps = block // rows
    tall = pl.BlockSpec((total, rows), lambda i, me_ref: (0, i))
    whole = pl.BlockSpec((total, hidden), lambda i, me_ref: (0, 0))
    out = pl.BlockSpec((rows, hidden), lambda i, me_ref: (i, 0))
    return pl.pallas_call(
        grad_kernel,
        grid_spec=pltpu.PrefetchScalarGridSpec(
            num_scalar_prefetch=1,
            grid=(steps,),
            in_specs=[
                tall,
                tall,
                whole,
                whole,
                pl.BlockSpec((rows, hidden), lambda i, me_ref: (me_ref[0] * steps + i, 0)),
                pl.BlockSpec((1, rows), lambda i, me_ref: (0, me_ref[0] * steps + i)),
            ],
            out_specs=[out, out, pl.BlockSpec((1, rows), lambda i, me_ref: (0, i))],
        ),
        out_shape=(
            jax.ShapeDtypeStruct((block, hidden), jnp.float32),
            jax.ShapeDtypeStruct((block, hidden), jnp.float32),
            jax.ShapeDtypeStruct((1, block), jnp.float32),
        ),
        compiler_params=pltpu.CompilerParams(vmem_limit_bytes=40 * 2**20),
    )(me, h, g, act, du, weight_in, gains)


def local(sections, replicas, inputs, cotangent, weight_in, weight_out, norm_gains):
    tokens, width = inputs.shape
    hidden = weight_in.shape[2]
    micros = tokens // ROWS
    count = 2 * micros
    block = width // replicas
    half = width // 2
    wide = jax.ShapeDtypeStruct((replicas, micros, ROWS, block), jnp.bfloat16)
    narrow = jax.ShapeDtypeStruct((replicas, micros, ROWS, hidden), jnp.bfloat16)
    any_spec = pl.BlockSpec(memory_space=pl.ANY)
    vmem_spec = pl.BlockSpec(memory_space=pltpu.VMEM)
    wide_scratch = pltpu.VMEM((count, ROWS, half), jnp.bfloat16)
    narrow_scratch = pltpu.VMEM((count, ROWS, hidden), jnp.bfloat16)
    sums_scratch = pltpu.VMEM((count, ROWS, hidden + 128), jnp.float32)
    rows_scratch = pltpu.VMEM((count, ROWS, hidden), jnp.float32)
    dma = pltpu.SemaphoreType.DMA
    all_h, all_g, all_act, all_du = pl.pallas_call(
        functools.partial(relay_kernel, sections, replicas, micros),
        out_shape=(wide, wide, narrow, narrow),
        in_specs=[any_spec] * 4 + [vmem_spec],
        out_specs=(any_spec,) * 4,
        scratch_shapes=[
            pltpu.VMEM((half, hidden), jnp.bfloat16),
            pltpu.VMEM((half, hidden), jnp.bfloat16),
            pltpu.VMEM((hidden, half), jnp.bfloat16),
            pltpu.VMEM((hidden, half), jnp.bfloat16),
            pltpu.VMEM((1, half), jnp.float32),
            wide_scratch,
            wide_scratch,
            wide_scratch,
            wide_scratch,
            narrow_scratch,
            narrow_scratch,
            rows_scratch,
            pltpu.VMEM((count, ROWS, 128), jnp.float32),
            sums_scratch,
            sums_scratch,
            rows_scratch,
            rows_scratch,
            dma((2, replicas // 2)),
            dma((count, 3)),
            dma((count, 3)),
            dma((count, 3)),
            dma((count, 3)),
            dma((count,)),
            dma((count,)),
            dma((3,)),
            dma((4,)),
            dma((4,)),
        ],
        compiler_params=pltpu.CompilerParams(
            collective_id=0, has_side_effects=True, vmem_limit_bytes=44 * 2**20
        ),
    )(
        inputs.reshape(micros, ROWS, width),
        cotangent.reshape(micros, ROWS, width),
        weight_in[0],
        weight_out[0],
        norm_gains,
    )
    total = replicas * tokens
    me = lax.axis_index("dp").astype(jnp.int32).reshape(1)
    in_grad, out_grad, gain_grad = gradients(
        me,
        all_h.reshape(total, block),
        all_g.reshape(total, block),
        all_act.reshape(total, hidden),
        all_du.reshape(total, hidden),
        weight_in[0],
        norm_gains,
    )
    return (in_grad[None], out_grad[None], gain_grad)


def solution(mesh):
    return jax.shard_map(
        functools.partial(local, mesh.shape["section"], mesh.shape["dp"]),
        mesh=mesh,
        in_specs=(
            P("dp", None),
            P("dp", None),
            P("section", None, None),
            P("section", None, None),
            P("section", None),
        ),
        out_specs=(P("section", "dp", None), P("section", "dp", None), P("section", "dp")),
        check_vma=False,
    )
```

```python
import functools

import jax
import jax.numpy as jnp
from jax import lax
from jax.experimental import pallas as pl
from jax.experimental.pallas import tpu as pltpu
from jax.sharding import PartitionSpec as P

ROWS = 16
LAG = 11
LAST_FINE = 2
EARLY = 2
EPSILON = 1e-05
MESH = pl.DeviceIdType.MESH


def dot(left, right):
    return jnp.dot(left, right, preferred_element_type=jnp.float32)


def nt_dot(left, right):
    return lax.dot_general(
        left, right, (((1,), (1,)), ((), ())), preferred_element_type=jnp.float32
    )


def relay_kernel(
    sections,
    replicas,
    micros,
    x_ref,
    c_ref,
    win_hbm,
    wout_hbm,
    gain_ref,
    all_h,
    all_g,
    all_act,
    all_du,
    win,
    wout,
    win_t,
    wout_t,
    gain,
    stash,
    up,
    out_f,
    out_b,
    act_buf,
    du_buf,
    pre,
    scale,
    fx_send,
    fx_recv,
    bx_send,
    bx_recv,
    w_sem,
    f_recv,
    b_recv,
    f_send,
    b_send,
    fx_sem,
    bx_sem,
    xs_sem,
    x_recv,
    x_send,
):
    half = stash.shape[2]
    width = 2 * half
    hidden = win.shape[1]
    count = 2 * micros
    block = width // replicas
    chips = replicas // 2
    quarter = half // 4
    pieces = ((0, quarter), (quarter, 2 * quarter), (3 * quarter, quarter))
    take = {True: ((0, 2), (2, 3)), False: ((0, 3),)}
    give = {True: ((0, 1), (1, 3)), False: ((0, 3),)}
    piece_of = [
        [k for k, (start, size) in enumerate(pieces) if start <= j * block < start + size][0]
        for j in range(chips)
    ]
    pos = lax.axis_index("section")
    me = lax.axis_index("dp")
    chip = me // 2
    core = lax.rem(me, 2)
    partner = me + 1 - 2 * core
    is_first = pos == 0
    is_last = pos == sections - 1
    not_first = pos > 0
    not_last = pos < sections - 1

    def part(owner):
        return pl.ds(pl.multiple_of(owner * block, block), block)

    def mine(j):
        return slice(j * block, (j + 1) * block)

    def span(first, past):
        start = pieces[first][0]
        return start, pieces[past - 1][0] + pieces[past - 1][1]

    def wcopy(kind, j):
        src, dst = ((win_hbm, win), (wout_hbm, wout))[kind]
        return pltpu.make_async_copy(
            src.at[part(2 * j + core), :], dst.at[mine(j), :], w_sem.at[kind, j]
        )

    def load_weights(kind):
        for j in range(chips):
            wcopy(kind, j).start()

    def load_own(src, dst, sems, m):
        for j in range(chips):
            pltpu.make_async_copy(
                src.at[m, :, part(2 * j + core)],
                dst.at[2 * m + core, :, mine(j)],
                sems.at[2 * m + core, piece_of[j]],
            ).start()

    def push_partner(src, dst, sems, m):
        for j in range(chips):
            pltpu.make_async_remote_copy(
                src_ref=src.at[m, :, part(2 * j + 1 - core)],
                dst_ref=dst.at[2 * m + core, :, mine(j)],
                send_sem=xs_sem.at[0],
                recv_sem=sems.at[2 * m + core, piece_of[j]],
                device_id={"dp": partner},
                device_id_type=MESH,
            ).start()

    def spread(src, dst, kind):
        @pl.loop(1, replicas)
        def _(step):
            peer = lax.rem(me + step, replicas)
            pltpu.make_async_remote_copy(
                src_ref=src.at[:, :, part(peer)],
                dst_ref=dst.at[me],
                send_sem=x_send.at[kind],
                recv_sem=x_recv.at[kind],
                device_id={"dp": peer},
                device_id_type=MESH,
            ).start()

    barrier = pltpu.get_barrier_semaphore()

    @pl.when(not_first)
    def _():
        pl.semaphore_signal(
            barrier, inc=1, device_id={"section": pos - 1}, device_id_type=MESH
        )

    @pl.when(not_last)
    def _():
        pl.semaphore_signal(
            barrier, inc=1, device_id={"section": pos + 1}, device_id_type=MESH
        )

    @pl.loop(1, replicas)
    def _(step):
        pl.semaphore_signal(
            barrier,
            inc=1,
            device_id={"dp": lax.rem(me + step, replicas)},
            device_id_type=MESH,
        )

    @pl.when(is_first)
    def _():
        load_own(x_ref, stash, f_recv, 0)
        load_weights(0)
        load_weights(1)

        @pl.loop(1, micros)
        def _(m):
            load_own(x_ref, stash, f_recv, m)

    @pl.when(not_first)
    def _():
        load_weights(1)
        load_weights(0)

    @pl.when(is_last)
    def _():
        @pl.loop(0, micros)
        def _(m):
            load_own(c_ref, up, b_recv, m)

    for j in range(chips):
        gain[:, mine(j)] = gain_ref[:, part(2 * j + core)]

    pl.semaphore_wait(
        barrier,
        replicas - 1 + not_first.astype(jnp.int32) + not_last.astype(jnp.int32),
    )

    @pl.when(is_first)
    def _():
        @pl.loop(0, EARLY)
        def _(m):
            push_partner(x_ref, stash, f_recv, m)

    @pl.when(is_last)
    def _():
        @pl.loop(0, micros)
        def _(m):
            push_partner(c_ref, up, b_recv, m)

        spread(c_ref, all_g, 2)

    @pl.when(not_first)
    def _():
        for j in range(chips):
            wcopy(1, j).wait()

            @pl.when(not_last)
            def _():
                wout_t[:, mine(j)] = wout[mine(j), :].T

        for j in range(chips):
            wcopy(0, j).wait()
            win_t[:, mine(j)] = win[mine(j), :].T

    def send_forward(i, k):
        start, size = pieces[k]
        return pltpu.make_async_remote_copy(
            src_ref=out_f.at[i, :, pl.ds(start, size)],
            dst_ref=stash.at[i, :, pl.ds(start, size)],
            send_sem=f_send.at[i, k],
            recv_sem=f_recv.at[i, k],
            device_id={"section": pos + 1},
            device_id_type=MESH,
        )

    def send_backward(i, k):
        start, size = pieces[k]
        return pltpu.make_async_remote_copy(
            src_ref=out_b.at[i, :, pl.ds(start, size)],
            dst_ref=up.at[i, :, pl.ds(start, size)],
            send_sem=b_send.at[i, k],
            recv_sem=b_recv.at[i, k],
            device_id={"section": pos - 1},
            device_id_type=MESH,
        )

    def trade_forward(i):
        return pltpu.make_async_remote_copy(
            src_ref=fx_send.at[i],
            dst_ref=fx_recv.at[i],
            send_sem=xs_sem.at[1],
            recv_sem=fx_sem.at[i],
            device_id={"dp": partner},
            device_id_type=MESH,
        )

    def trade_backward(i):
        return pltpu.make_async_remote_copy(
            src_ref=bx_send.at[i],
            dst_ref=bx_recv.at[i],
            send_sem=xs_sem.at[2],
            recv_sem=bx_sem.at[i],
            device_id={"dp": partner},
            device_id_type=MESH,
        )

    def arrived(buffer, sems, i, first, past):
        for k in range(first, past):
            start, size = pieces[k]
            piece = buffer.at[i, :, pl.ds(start, size)]
            pltpu.make_async_copy(piece, piece, sems.at[i, k]).wait()

    def share(kind, i, src_of, dst):
        slot = dst.at[2 * chip + lax.rem(i, 2), i // 2]
        pltpu.make_async_copy(src_of(chip), slot, x_recv.at[kind]).start()
        for step in range(1, chips):
            target = lax.rem(chip + step, chips)
            pltpu.make_async_remote_copy(
                src_ref=src_of(target),
                dst_ref=slot,
                send_sem=x_send.at[kind],
                recv_sem=x_recv.at[kind],
                device_id={"dp": 2 * target + core},
                device_id_type=MESH,
            ).start()

    def keep_own(kind, i, src, dst):
        @pl.when(lax.rem(i, 2) == core)
        def _():
            pltpu.make_async_copy(
                src.at[i, :, part(chip)], dst.at[me, i // 2], x_recv.at[kind]
            ).start()

    def forward_in(i, fine):
        total = jnp.zeros((ROWS, 1), jnp.float32)
        u = jnp.zeros((ROWS, hidden), jnp.float32)
        for first, past in take[fine]:
            start, stop = span(first, past)
            arrived(stash, f_recv, i, first, past)

            if fine:

                @pl.when((i == 0) & is_first)
                def _():
                    for j in range(chips):
                        if start <= j * block < stop:
                            wcopy(0, j).wait()

            h = stash[i, :, start:stop].astype(jnp.float32)
            scaled = (h * gain[:, start:stop]).astype(jnp.bfloat16)
            total = total + jnp.sum(h * h, axis=1, keepdims=True)
            u = u + dot(scaled, win[start:stop, :])
        fx_send[i, :, :hidden] = u
        fx_send[i, :, hidden:] = jnp.broadcast_to(total, (ROWS, 128))
        trade_forward(i).start()

        @pl.when(is_first)
        def _():
            keep_own(0, i, stash, all_h)

        @pl.when(not_first)
        def _():
            share(0, i, lambda j: stash.at[i, :, part(j)], all_h)

    def forward_out(i, fine):
        pltpu.make_async_copy(fx_recv.at[i], fx_recv.at[i], fx_sem.at[i]).wait()
        total = fx_send[i, :, hidden:] + fx_recv[i, :, hidden:]
        inv = lax.rsqrt(total / width + EPSILON)
        scale[i] = inv
        u = (fx_send[i, :, :hidden] + fx_recv[i, :, :hidden]) * inv[:, :1]
        act = (u * jax.nn.sigmoid(u)).astype(jnp.bfloat16)
        pre[i] = u
        act_buf[i] = act

        if fine:

            @pl.when((i == 0) & is_first)
            def _():
                for j in range(chips):
                    wcopy(1, j).wait()

        def emit(product):
            for first, past in give[fine]:
                start, stop = span(first, past)
                h = stash[i, :, start:stop].astype(jnp.float32)
                out_f[i, :, start:stop] = (h + product(act, start, stop)).astype(
                    jnp.bfloat16
                )
                for k in range(first, past):
                    send_forward(i, k).start()

        if fine:

            @pl.when(is_first)
            def _():
                emit(lambda a, start, stop: nt_dot(a, wout[start:stop, :]))

        @pl.when(not_first & not_last)
        def _():
            emit(lambda a, start, stop: dot(a, wout_t[:, start:stop]))

        share(1, i, lambda j: act_buf.at[i], all_act)

    def backward_in(i, fine):
        da = jnp.zeros((ROWS, hidden), jnp.float32)
        for first, past in take[fine]:
            start, stop = span(first, past)
            arrived(up, b_recv, i, first, past)
            da = da + dot(up[i, :, start:stop], wout[start:stop, :])
        bx_send[i] = da
        trade_backward(i).start()

        @pl.when(is_last)
        def _():
            keep_own(2, i, up, all_g)

        @pl.when(not_last)
        def _():
            share(2, i, lambda j: up.at[i, :, part(j)], all_g)

    def backward_out(i, fine):
        pltpu.make_async_copy(bx_recv.at[i], bx_recv.at[i], bx_sem.at[i]).wait()
        da = bx_send[i] + bx_recv[i]
        u = pre[i]
        inv = scale[i][:, :1]
        sig = jax.nn.sigmoid(u)
        wide_du = da * sig * (1.0 + u * (1.0 - sig))
        du = wide_du.astype(jnp.bfloat16)
        du_buf[i] = (wide_du * inv).astype(jnp.bfloat16)

        @pl.when(not_first)
        def _():
            centered = jnp.sum(du.astype(jnp.float32) * u, axis=1, keepdims=True) / (
                inv * width
            )
            pull = inv * inv * inv * centered
            for first, past in give[fine]:
                start, stop = span(first, past)
                h = stash[i, :, start:stop].astype(jnp.float32)
                g = up[i, :, start:stop].astype(jnp.float32)
                dn = dot(du, win_t[:, start:stop])
                out_b[i, :, start:stop] = (
                    g + inv * (dn * gain[:, start:stop]) - h * pull
                ).astype(jnp.bfloat16)
                for k in range(first, past):
                    send_backward(i, k).start()

        share(3, i, lambda j: du_buf.at[i], all_du)

    lag = jnp.minimum(LAG * (sections - 1 - pos) // 2, count)
    lag = jnp.where(is_first, count, lag)
    lead = is_first.astype(jnp.int32)

    @pl.loop(0, count + lag)
    def _(step):
        ahead = step - lead
        back = step - lag
        both = (back >= 0) & (step < count)
        last = (step >= count) & (back >= count - LAST_FINE)

        @pl.when(both)
        def _():
            forward_in(step, False)
            backward_in(back, False)
            forward_out(step, False)
            backward_out(back, False)

        @pl.when((step < count) & (back < 0))
        def _():
            forward_in(step, True)

            later = step // 2 + EARLY

            @pl.when(is_first & (lax.rem(step, 2) == 0) & (later < micros))
            def _():
                push_partner(x_ref, stash, f_recv, later)

            @pl.when(is_first & (step == 1))
            def _():
                spread(x_ref, all_h, 0)

        @pl.when((ahead >= 0) & (ahead < count) & (ahead < lag))
        def _():
            forward_out(ahead, True)

        @pl.when((step >= count) & jnp.logical_not(last))
        def _():
            backward_in(back, False)
            backward_out(back, False)

        @pl.when(last)
        def _():
            backward_in(back, True)
            backward_out(back, True)

    @pl.loop(0, count)
    def _(i):
        for k in range(len(pieces)):

            @pl.when(not_last)
            def _():
                send_forward(i, k).wait_send()

            @pl.when(not_first)
            def _():
                send_backward(i, k).wait_send()

    def drain(ref, sem):
        pltpu.make_async_copy(ref, ref, sem).wait()

    @pl.when(is_first | is_last)
    def _():
        drain(stash.at[pl.ds(0, micros)], xs_sem.at[0])

    drain(fx_send, xs_sem.at[1])
    drain(bx_send, xs_sem.at[2])
    for kind, ref, early in (
        (0, all_h, is_first),
        (1, all_act, False),
        (2, all_g, is_last),
        (3, all_du, False),
    ):
        drain(ref.at[pl.ds(0, replicas - 2)], x_send.at[kind])
        if early is not False:

            @pl.when(early)
            def _():
                drain(ref.at[0], x_send.at[kind])

        drain(ref, x_recv.at[kind])


def grad_kernel(me_ref, h_ref, g_ref, act_ref, du_ref, win_ref, gain_ref, din, dout, dgain):
    raw = jnp.dot(h_ref[...].T, du_ref[...], preferred_element_type=jnp.float32)
    rows = raw.shape[0]
    gain = jnp.broadcast_to(gain_ref[...], (128, rows)).T[:, :1]
    din[...] = raw * gain
    sums = jnp.sum(win_ref[...].astype(jnp.float32) * raw, axis=1, keepdims=True)
    dgain[...] = jnp.broadcast_to(sums, (rows, 128)).T[:1]
    dout[...] = jnp.dot(g_ref[...].T, act_ref[...], preferred_element_type=jnp.float32)


def gradients(me, h, g, act, du, weight_in, gains):
    total, block = h.shape
    hidden = act.shape[1]
    rows = min(512, block)
    steps = block // rows
    tall = pl.BlockSpec((total, rows), lambda i, me_ref: (0, i))
    whole = pl.BlockSpec((total, hidden), lambda i, me_ref: (0, 0))
    out = pl.BlockSpec((rows, hidden), lambda i, me_ref: (i, 0))
    return pl.pallas_call(
        grad_kernel,
        grid_spec=pltpu.PrefetchScalarGridSpec(
            num_scalar_prefetch=1,
            grid=(steps,),
            in_specs=[
                tall,
                tall,
                whole,
                whole,
                pl.BlockSpec((rows, hidden), lambda i, me_ref: (me_ref[0] * steps + i, 0)),
                pl.BlockSpec((1, rows), lambda i, me_ref: (0, me_ref[0] * steps + i)),
            ],
            out_specs=[out, out, pl.BlockSpec((1, rows), lambda i, me_ref: (0, i))],
        ),
        out_shape=(
            jax.ShapeDtypeStruct((block, hidden), jnp.float32),
            jax.ShapeDtypeStruct((block, hidden), jnp.float32),
            jax.ShapeDtypeStruct((1, block), jnp.float32),
        ),
        compiler_params=pltpu.CompilerParams(vmem_limit_bytes=40 * 2**20),
    )(me, h, g, act, du, weight_in, gains)


def local(sections, replicas, inputs, cotangent, weight_in, weight_out, norm_gains):
    tokens, width = inputs.shape
    hidden = weight_in.shape[2]
    micros = tokens // ROWS
    count = 2 * micros
    block = width // replicas
    half = width // 2
    wide = jax.ShapeDtypeStruct((replicas, micros, ROWS, block), jnp.bfloat16)
    narrow = jax.ShapeDtypeStruct((replicas, micros, ROWS, hidden), jnp.bfloat16)
    any_spec = pl.BlockSpec(memory_space=pl.ANY)
    vmem_spec = pl.BlockSpec(memory_space=pltpu.VMEM)
    wide_scratch = pltpu.VMEM((count, ROWS, half), jnp.bfloat16)
    narrow_scratch = pltpu.VMEM((count, ROWS, hidden), jnp.bfloat16)
    sums_scratch = pltpu.VMEM((count, ROWS, hidden + 128), jnp.float32)
    rows_scratch = pltpu.VMEM((count, ROWS, hidden), jnp.float32)
    dma = pltpu.SemaphoreType.DMA
    all_h, all_g, all_act, all_du = pl.pallas_call(
        functools.partial(relay_kernel, sections, replicas, micros),
        out_shape=(wide, wide, narrow, narrow),
        in_specs=[any_spec] * 4 + [vmem_spec],
        out_specs=(any_spec,) * 4,
        scratch_shapes=[
            pltpu.VMEM((half, hidden), jnp.bfloat16),
            pltpu.VMEM((half, hidden), jnp.bfloat16),
            pltpu.VMEM((hidden, half), jnp.bfloat16),
            pltpu.VMEM((hidden, half), jnp.bfloat16),
            pltpu.VMEM((1, half), jnp.float32),
            wide_scratch,
            wide_scratch,
            wide_scratch,
            wide_scratch,
            narrow_scratch,
            narrow_scratch,
            rows_scratch,
            pltpu.VMEM((count, ROWS, 128), jnp.float32),
            sums_scratch,
            sums_scratch,
            rows_scratch,
            rows_scratch,
            dma((2, replicas // 2)),
            dma((count, 3)),
            dma((count, 3)),
            dma((count, 3)),
            dma((count, 3)),
            dma((count,)),
            dma((count,)),
            dma((3,)),
            dma((4,)),
            dma((4,)),
        ],
        compiler_params=pltpu.CompilerParams(
            collective_id=0, has_side_effects=True, vmem_limit_bytes=44 * 2**20
        ),
    )(
        inputs.reshape(micros, ROWS, width),
        cotangent.reshape(micros, ROWS, width),
        weight_in[0],
        weight_out[0],
        norm_gains,
    )
    total = replicas * tokens
    me = lax.axis_index("dp").astype(jnp.int32).reshape(1)
    in_grad, out_grad, gain_grad = gradients(
        me,
        all_h.reshape(total, block),
        all_g.reshape(total, block),
        all_act.reshape(total, hidden),
        all_du.reshape(total, hidden),
        weight_in[0],
        norm_gains,
    )
    return (in_grad[None], out_grad[None], gain_grad)


def solution(mesh):
    return jax.shard_map(
        functools.partial(local, mesh.shape["section"], mesh.shape["dp"]),
        mesh=mesh,
        in_specs=(
            P("dp", None),
            P("dp", None),
            P("section", None, None),
            P("section", None, None),
            P("section", None),
        ),
        out_specs=(P("section", "dp", None), P("section", "dp", None), P("section", "dp")),
        check_vma=False,
    )
```

```python
import functools

import jax
import jax.numpy as jnp
from jax import lax
from jax.experimental import pallas as pl
from jax.experimental.pallas import tpu as pltpu
from jax.sharding import PartitionSpec as P

ROWS = 16
LAG = 10
LAST_FINE = 2
EARLY = 2
EPSILON = 1e-05
MESH = pl.DeviceIdType.MESH


def dot(left, right):
    return jnp.dot(left, right, preferred_element_type=jnp.float32)


def nt_dot(left, right):
    return lax.dot_general(
        left, right, (((1,), (1,)), ((), ())), preferred_element_type=jnp.float32
    )


def relay_kernel(
    sections,
    replicas,
    micros,
    x_ref,
    c_ref,
    win_hbm,
    wout_hbm,
    gain_ref,
    all_h,
    all_g,
    all_act,
    all_du,
    win,
    wout,
    win_t,
    wout_t,
    gain,
    stash,
    up,
    out_f,
    out_b,
    act_buf,
    du_buf,
    pre,
    scale,
    fx_send,
    fx_recv,
    bx_send,
    bx_recv,
    w_sem,
    f_recv,
    b_recv,
    f_send,
    b_send,
    fx_sem,
    bx_sem,
    xs_sem,
    x_recv,
    x_send,
):
    half = stash.shape[2]
    width = 2 * half
    hidden = win.shape[1]
    count = 2 * micros
    block = width // replicas
    chips = replicas // 2
    quarter = half // 4
    pieces = ((0, quarter), (quarter, 2 * quarter), (3 * quarter, quarter))
    take = {True: ((0, 2), (2, 3)), False: ((0, 3),)}
    give = {True: ((0, 1), (1, 3)), False: ((0, 3),)}
    piece_of = [
        [k for k, (start, size) in enumerate(pieces) if start <= j * block < start + size][0]
        for j in range(chips)
    ]
    pos = lax.axis_index("section")
    me = lax.axis_index("dp")
    chip = me // 2
    core = lax.rem(me, 2)
    partner = me + 1 - 2 * core
    is_first = pos == 0
    is_last = pos == sections - 1
    not_first = pos > 0
    not_last = pos < sections - 1

    def part(owner):
        return pl.ds(pl.multiple_of(owner * block, block), block)

    def mine(j):
        return slice(j * block, (j + 1) * block)

    def span(first, past):
        start = pieces[first][0]
        return start, pieces[past - 1][0] + pieces[past - 1][1]

    def wcopy(kind, j):
        src, dst = ((win_hbm, win), (wout_hbm, wout))[kind]
        return pltpu.make_async_copy(
            src.at[part(2 * j + core), :], dst.at[mine(j), :], w_sem.at[kind, j]
        )

    def load_weights(kind):
        for j in range(chips):
            wcopy(kind, j).start()

    def load_own(src, dst, sems, m):
        for j in range(chips):
            pltpu.make_async_copy(
                src.at[m, :, part(2 * j + core)],
                dst.at[2 * m + core, :, mine(j)],
                sems.at[2 * m + core, piece_of[j]],
            ).start()

    def push_partner(src, dst, sems, m):
        for j in range(chips):
            pltpu.make_async_remote_copy(
                src_ref=src.at[m, :, part(2 * j + 1 - core)],
                dst_ref=dst.at[2 * m + core, :, mine(j)],
                send_sem=xs_sem.at[0],
                recv_sem=sems.at[2 * m + core, piece_of[j]],
                device_id={"dp": partner},
                device_id_type=MESH,
            ).start()

    def spread(src, dst, kind):
        @pl.loop(1, replicas)
        def _(step):
            peer = lax.rem(me + step, replicas)
            pltpu.make_async_remote_copy(
                src_ref=src.at[:, :, part(peer)],
                dst_ref=dst.at[me],
                send_sem=x_send.at[kind],
                recv_sem=x_recv.at[kind],
                device_id={"dp": peer},
                device_id_type=MESH,
            ).start()

    barrier = pltpu.get_barrier_semaphore()

    @pl.when(not_first)
    def _():
        pl.semaphore_signal(
            barrier, inc=1, device_id={"section": pos - 1}, device_id_type=MESH
        )

    @pl.when(not_last)
    def _():
        pl.semaphore_signal(
            barrier, inc=1, device_id={"section": pos + 1}, device_id_type=MESH
        )

    @pl.loop(1, replicas)
    def _(step):
        pl.semaphore_signal(
            barrier,
            inc=1,
            device_id={"dp": lax.rem(me + step, replicas)},
            device_id_type=MESH,
        )

    @pl.when(is_first)
    def _():
        load_own(x_ref, stash, f_recv, 0)
        load_weights(0)
        load_weights(1)

        @pl.loop(1, micros)
        def _(m):
            load_own(x_ref, stash, f_recv, m)

    @pl.when(not_first)
    def _():
        load_weights(1)
        load_weights(0)

    @pl.when(is_last)
    def _():
        @pl.loop(0, micros)
        def _(m):
            load_own(c_ref, up, b_recv, m)

    def gain_copy(j):
        return pltpu.make_async_copy(
            gain_ref.at[:, part(2 * j + core)], gain.at[:, mine(j)], w_sem.at[2, j]
        )

    for j in range(chips):
        gain_copy(j).start()

    pl.semaphore_wait(
        barrier,
        replicas - 1 + not_first.astype(jnp.int32) + not_last.astype(jnp.int32),
    )

    @pl.when(is_first)
    def _():
        @pl.loop(0, EARLY)
        def _(m):
            push_partner(x_ref, stash, f_recv, m)

    @pl.when(is_last)
    def _():
        @pl.loop(0, micros)
        def _(m):
            push_partner(c_ref, up, b_recv, m)

        spread(c_ref, all_g, 2)

    @pl.when(not_first)
    def _():
        for j in range(chips):
            wcopy(1, j).wait()

            @pl.when(not_last)
            def _():
                wout_t[:, mine(j)] = wout[mine(j), :].T

        for j in range(chips):
            wcopy(0, j).wait()
            win_t[:, mine(j)] = win[mine(j), :].T

    for j in range(chips):
        gain_copy(j).wait()

    def send_forward(i, k):
        start, size = pieces[k]
        return pltpu.make_async_remote_copy(
            src_ref=out_f.at[i, :, pl.ds(start, size)],
            dst_ref=stash.at[i, :, pl.ds(start, size)],
            send_sem=f_send.at[i, k],
            recv_sem=f_recv.at[i, k],
            device_id={"section": pos + 1},
            device_id_type=MESH,
        )

    def send_backward(i, k):
        start, size = pieces[k]
        return pltpu.make_async_remote_copy(
            src_ref=out_b.at[i, :, pl.ds(start, size)],
            dst_ref=up.at[i, :, pl.ds(start, size)],
            send_sem=b_send.at[i, k],
            recv_sem=b_recv.at[i, k],
            device_id={"section": pos - 1},
            device_id_type=MESH,
        )

    def trade_forward(i):
        return pltpu.make_async_remote_copy(
            src_ref=fx_send.at[i],
            dst_ref=fx_recv.at[i],
            send_sem=xs_sem.at[1],
            recv_sem=fx_sem.at[i],
            device_id={"dp": partner},
            device_id_type=MESH,
        )

    def trade_backward(i):
        return pltpu.make_async_remote_copy(
            src_ref=bx_send.at[i],
            dst_ref=bx_recv.at[i],
            send_sem=xs_sem.at[2],
            recv_sem=bx_sem.at[i],
            device_id={"dp": partner},
            device_id_type=MESH,
        )

    def arrived(buffer, sems, i, first, past):
        for k in range(first, past):
            start, size = pieces[k]
            piece = buffer.at[i, :, pl.ds(start, size)]
            pltpu.make_async_copy(piece, piece, sems.at[i, k]).wait()

    def share(kind, i, src_of, dst):
        slot = dst.at[2 * chip + lax.rem(i, 2), i // 2]
        pltpu.make_async_copy(src_of(chip), slot, x_recv.at[kind]).start()
        for step in range(1, chips):
            target = lax.rem(chip + step, chips)
            pltpu.make_async_remote_copy(
                src_ref=src_of(target),
                dst_ref=slot,
                send_sem=x_send.at[kind],
                recv_sem=x_recv.at[kind],
                device_id={"dp": 2 * target + core},
                device_id_type=MESH,
            ).start()

    def keep_own(kind, i, src, dst):
        @pl.when(lax.rem(i, 2) == core)
        def _():
            pltpu.make_async_copy(
                src.at[i, :, part(chip)], dst.at[me, i // 2], x_recv.at[kind]
            ).start()

    def forward_in(i, fine):
        total = jnp.zeros((ROWS, 1), jnp.float32)
        u = jnp.zeros((ROWS, hidden), jnp.float32)
        for first, past in take[fine]:
            start, stop = span(first, past)
            arrived(stash, f_recv, i, first, past)

            if fine:

                @pl.when((i == 0) & is_first)
                def _():
                    for j in range(chips):
                        if start <= j * block < stop:
                            wcopy(0, j).wait()

            h = stash[i, :, start:stop].astype(jnp.float32)
            scaled = (h * gain[:, start:stop]).astype(jnp.bfloat16)
            total = total + jnp.sum(h * h, axis=1, keepdims=True)
            u = u + dot(scaled, win[start:stop, :])
        fx_send[i, :, :hidden] = u
        fx_send[i, :, hidden:] = jnp.broadcast_to(total, (ROWS, 128))
        trade_forward(i).start()

        @pl.when(is_first)
        def _():
            keep_own(0, i, stash, all_h)

        @pl.when(not_first)
        def _():
            share(0, i, lambda j: stash.at[i, :, part(j)], all_h)

    def forward_out(i, fine):
        pltpu.make_async_copy(fx_recv.at[i], fx_recv.at[i], fx_sem.at[i]).wait()
        total = fx_send[i, :, hidden:] + fx_recv[i, :, hidden:]
        inv = lax.rsqrt(total / width + EPSILON)
        scale[i] = inv
        u = (fx_send[i, :, :hidden] + fx_recv[i, :, :hidden]) * inv[:, :1]
        act = (u * jax.nn.sigmoid(u)).astype(jnp.bfloat16)
        pre[i] = u
        act_buf[i] = act

        if fine:

            @pl.when((i == 0) & is_first)
            def _():
                for j in range(chips):
                    wcopy(1, j).wait()

        def emit(product):
            for first, past in give[fine]:
                start, stop = span(first, past)
                h = stash[i, :, start:stop].astype(jnp.float32)
                out_f[i, :, start:stop] = (h + product(act, start, stop)).astype(
                    jnp.bfloat16
                )
                for k in range(first, past):
                    send_forward(i, k).start()

        if fine:

            @pl.when(is_first)
            def _():
                emit(lambda a, start, stop: nt_dot(a, wout[start:stop, :]))

        @pl.when(not_first & not_last)
        def _():
            emit(lambda a, start, stop: dot(a, wout_t[:, start:stop]))

        share(1, i, lambda j: act_buf.at[i], all_act)

    def backward_in(i, fine):
        da = jnp.zeros((ROWS, hidden), jnp.float32)
        for first, past in take[fine]:
            start, stop = span(first, past)
            arrived(up, b_recv, i, first, past)
            da = da + dot(up[i, :, start:stop], wout[start:stop, :])
        bx_send[i] = da
        trade_backward(i).start()

        @pl.when(is_last)
        def _():
            keep_own(2, i, up, all_g)

        @pl.when(not_last)
        def _():
            share(2, i, lambda j: up.at[i, :, part(j)], all_g)

    def backward_out(i, fine):
        pltpu.make_async_copy(bx_recv.at[i], bx_recv.at[i], bx_sem.at[i]).wait()
        da = bx_send[i] + bx_recv[i]
        u = pre[i]
        inv = scale[i][:, :1]
        sig = jax.nn.sigmoid(u)
        wide_du = da * sig * (1.0 + u * (1.0 - sig))
        du = wide_du.astype(jnp.bfloat16)
        du_buf[i] = (wide_du * inv).astype(jnp.bfloat16)

        @pl.when(not_first)
        def _():
            centered = jnp.sum(du.astype(jnp.float32) * u, axis=1, keepdims=True) / (
                inv * width
            )
            pull = inv * inv * inv * centered
            for first, past in give[fine]:
                start, stop = span(first, past)
                h = stash[i, :, start:stop].astype(jnp.float32)
                g = up[i, :, start:stop].astype(jnp.float32)
                dn = dot(du, win_t[:, start:stop])
                out_b[i, :, start:stop] = (
                    g + inv * (dn * gain[:, start:stop]) - h * pull
                ).astype(jnp.bfloat16)
                for k in range(first, past):
                    send_backward(i, k).start()

        share(3, i, lambda j: du_buf.at[i], all_du)

    lag = jnp.minimum(LAG * (sections - 1 - pos) // 2, count)
    lag = jnp.where(is_first, count, lag)
    lead = is_first.astype(jnp.int32)

    @pl.when(is_last)
    def _():
        @pl.loop(0, count)
        def _(i):
            backward_in(i, False)

    @pl.loop(0, count + lag)
    def _(step):
        ahead = step - lead
        back = step - lag
        both = (back >= 0) & (step < count)
        last = (step >= count) & (back >= count - LAST_FINE)

        @pl.when(both)
        def _():
            forward_in(step, False)

            @pl.when(not_last)
            def _():
                backward_in(back, False)

            forward_out(step, False)
            backward_out(back, False)

        @pl.when((step < count) & (back < 0))
        def _():
            forward_in(step, True)

            later = step // 2 + EARLY

            @pl.when(is_first & (lax.rem(step, 2) == 0) & (later < micros))
            def _():
                push_partner(x_ref, stash, f_recv, later)

            @pl.when(is_first & (step == 1))
            def _():
                spread(x_ref, all_h, 0)

        @pl.when((ahead >= 0) & (ahead < count) & (ahead < lag))
        def _():
            forward_out(ahead, True)

        @pl.when((step >= count) & jnp.logical_not(last))
        def _():
            backward_in(back, False)
            backward_out(back, False)

        @pl.when(last)
        def _():
            backward_in(back, True)
            backward_out(back, True)

    @pl.loop(0, count)
    def _(i):
        for k in range(len(pieces)):

            @pl.when(not_last)
            def _():
                send_forward(i, k).wait_send()

            @pl.when(not_first)
            def _():
                send_backward(i, k).wait_send()

    def drain(ref, sem):
        pltpu.make_async_copy(ref, ref, sem).wait()

    @pl.when(is_first | is_last)
    def _():
        drain(stash.at[pl.ds(0, micros)], xs_sem.at[0])

    drain(fx_send, xs_sem.at[1])
    drain(bx_send, xs_sem.at[2])
    for kind, ref, early in (
        (0, all_h, is_first),
        (1, all_act, False),
        (2, all_g, is_last),
        (3, all_du, False),
    ):
        drain(ref.at[pl.ds(0, replicas - 2)], x_send.at[kind])
        if early is not False:

            @pl.when(early)
            def _():
                drain(ref.at[0], x_send.at[kind])

        drain(ref, x_recv.at[kind])


def grad_kernel(me_ref, h_ref, g_ref, act_ref, du_ref, win_ref, gain_ref, din, dout, dgain):
    raw = jnp.dot(h_ref[...].T, du_ref[...], preferred_element_type=jnp.float32)
    rows = raw.shape[0]
    gain = jnp.broadcast_to(gain_ref[...], (128, rows)).T[:, :1]
    din[...] = raw * gain
    sums = jnp.sum(win_ref[...].astype(jnp.float32) * raw, axis=1, keepdims=True)
    dgain[...] = jnp.broadcast_to(sums, (rows, 128)).T[:1]
    dout[...] = jnp.dot(g_ref[...].T, act_ref[...], preferred_element_type=jnp.float32)


def gradients(me, h, g, act, du, weight_in, gains):
    total, block = h.shape
    hidden = act.shape[1]
    rows = min(512, block)
    steps = block // rows
    tall = pl.BlockSpec((total, rows), lambda i, me_ref: (0, i))
    whole = pl.BlockSpec((total, hidden), lambda i, me_ref: (0, 0))
    out = pl.BlockSpec((rows, hidden), lambda i, me_ref: (i, 0))
    return pl.pallas_call(
        grad_kernel,
        grid_spec=pltpu.PrefetchScalarGridSpec(
            num_scalar_prefetch=1,
            grid=(steps,),
            in_specs=[
                tall,
                tall,
                whole,
                whole,
                pl.BlockSpec((rows, hidden), lambda i, me_ref: (me_ref[0] * steps + i, 0)),
                pl.BlockSpec((1, rows), lambda i, me_ref: (0, me_ref[0] * steps + i)),
            ],
            out_specs=[out, out, pl.BlockSpec((1, rows), lambda i, me_ref: (0, i))],
        ),
        out_shape=(
            jax.ShapeDtypeStruct((block, hidden), jnp.float32),
            jax.ShapeDtypeStruct((block, hidden), jnp.float32),
            jax.ShapeDtypeStruct((1, block), jnp.float32),
        ),
        compiler_params=pltpu.CompilerParams(vmem_limit_bytes=40 * 2**20),
    )(me, h, g, act, du, weight_in, gains)


def local(sections, replicas, inputs, cotangent, weight_in, weight_out, norm_gains):
    tokens, width = inputs.shape
    hidden = weight_in.shape[2]
    micros = tokens // ROWS
    count = 2 * micros
    block = width // replicas
    half = width // 2
    wide = jax.ShapeDtypeStruct((replicas, micros, ROWS, block), jnp.bfloat16)
    narrow = jax.ShapeDtypeStruct((replicas, micros, ROWS, hidden), jnp.bfloat16)
    any_spec = pl.BlockSpec(memory_space=pl.ANY)
    wide_scratch = pltpu.VMEM((count, ROWS, half), jnp.bfloat16)
    narrow_scratch = pltpu.VMEM((count, ROWS, hidden), jnp.bfloat16)
    sums_scratch = pltpu.VMEM((count, ROWS, hidden + 128), jnp.float32)
    rows_scratch = pltpu.VMEM((count, ROWS, hidden), jnp.float32)
    dma = pltpu.SemaphoreType.DMA
    all_h, all_g, all_act, all_du = pl.pallas_call(
        functools.partial(relay_kernel, sections, replicas, micros),
        out_shape=(wide, wide, narrow, narrow),
        in_specs=[any_spec] * 5,
        out_specs=(any_spec,) * 4,
        scratch_shapes=[
            pltpu.VMEM((half, hidden), jnp.bfloat16),
            pltpu.VMEM((half, hidden), jnp.bfloat16),
            pltpu.VMEM((hidden, half), jnp.bfloat16),
            pltpu.VMEM((hidden, half), jnp.bfloat16),
            pltpu.VMEM((1, half), jnp.float32),
            wide_scratch,
            wide_scratch,
            wide_scratch,
            wide_scratch,
            narrow_scratch,
            narrow_scratch,
            rows_scratch,
            pltpu.VMEM((count, ROWS, 128), jnp.float32),
            sums_scratch,
            sums_scratch,
            rows_scratch,
            rows_scratch,
            dma((3, replicas // 2)),
            dma((count, 3)),
            dma((count, 3)),
            dma((count, 3)),
            dma((count, 3)),
            dma((count,)),
            dma((count,)),
            dma((3,)),
            dma((4,)),
            dma((4,)),
        ],
        compiler_params=pltpu.CompilerParams(
            collective_id=0, has_side_effects=True, vmem_limit_bytes=44 * 2**20
        ),
    )(
        inputs.reshape(micros, ROWS, width),
        cotangent.reshape(micros, ROWS, width),
        weight_in[0],
        weight_out[0],
        norm_gains,
    )
    total = replicas * tokens
    me = lax.axis_index("dp").astype(jnp.int32).reshape(1)
    in_grad, out_grad, gain_grad = gradients(
        me,
        all_h.reshape(total, block),
        all_g.reshape(total, block),
        all_act.reshape(total, hidden),
        all_du.reshape(total, hidden),
        weight_in[0],
        norm_gains,
    )
    return (in_grad[None], out_grad[None], gain_grad)


def solution(mesh):
    return jax.shard_map(
        functools.partial(local, mesh.shape["section"], mesh.shape["dp"]),
        mesh=mesh,
        in_specs=(
            P("dp", None),
            P("dp", None),
            P("section", None, None),
            P("section", None, None),
            P("section", None),
        ),
        out_specs=(P("section", "dp", None), P("section", "dp", None), P("section", "dp")),
        check_vma=False,
    )
```
